512 devices in a mesh: rows: 128 (over z, y, core), help: 4 (over x).
Axes of the slice: x: 4, y: 4, z: 16, core: 2. Of those that a mesh axis runs over, the one named last changes fastest.
Arguments:
- embeddings: float32 [131072, 768], P(('rows', 'help')), may hold values from -40 to 40
- cluster_ids: int32 [131072], P(('rows', 'help')), may hold values from 0 to 511, as said below
- orders: int32 [131072], P(('rows', 'help')), may hold values from 0 to 1023, as said below
- owner: int32 [512], replicated, may hold values from 0 to 511, each once
Outputs:
- centroids: float32 [512, 768], P(('rows', 'help'))
- max_cosine: float32 [131072], P(('rows', 'help'))
- center_cosine: float32 [131072], P(('rows', 'help'))
The draws below stay inside these ranges and needn't reach their ends.
Inputs may be any that keep to these rules, and one draw needn't show every extreme that they name: `cluster_ids`: among the 256 rows of one device no cluster appears more than 2 times; one cluster appears exactly 2 times on every device; every cluster has at least one row. Within each cluster the orders of its rows are distinct and run from 0 to its number of rows minus 1. `owner`: each device index appears exactly once.
All inputs are finite; a program needn't handle non-finite values.
Results may differ from the reference program's by a relative error of at most 0.007.
Values may be sent and summed in bfloat16 or wider, within the bound.
No kernel may reach another device: no remote copies, remote signals or barrier semaphores. Data moves between devices by JAX's collectives and lax.ppermute only.
A program may use at most 64 MiB of HBM per device.

```python
import jax
import jax.numpy as jnp
from jax import lax

D = 768
R_DEV = 256
K = 512
CAP = 2
ROWS_ALL = 131072


def cluster_layout(key):
    base_key = jax.random.fold_in(key, 7001)
    pick_key, weight_key, forced_key, block_key = jax.random.split(base_key, 4)
    heavy_cluster = jax.random.randint(pick_key, (), 0, K)
    others = (heavy_cluster + 1 + jnp.arange(K - 1, dtype=jnp.int32)) % K
    weights = jax.random.randint(weight_key, (K - 1,), 1, 5)
    pool_cluster = jnp.repeat(others, CAP)
    pool_weight = jnp.repeat(weights, CAP)
    forced = jax.random.permutation(forced_key, K - 1)
    entries = jnp.arange((K - 1) * CAP, dtype=jnp.int32)

    def one_block(block_number, block_rng):
        score_key, order_key = jax.random.split(block_rng)
        raw_score = jax.random.randint(score_key, ((K - 1) * CAP,), 0, 1024) * pool_weight
        scores = raw_score * (4 * R_DEV) + entries
        chosen_entry = forced[block_number % (K - 1)] * CAP
        scores = jnp.where(entries == chosen_entry, 1 << 30, scores)
        picked = lax.top_k(scores, R_DEV - CAP)[1]
        block_ids = jnp.concatenate([jnp.full((CAP,), heavy_cluster, jnp.int32), pool_cluster[picked].astype(jnp.int32)])
        return block_ids[jax.random.permutation(order_key, R_DEV)]
    block_keys = jax.random.split(block_key, K)
    return jax.vmap(one_block)(jnp.arange(K, dtype=jnp.int32), block_keys).reshape(-1).astype(jnp.int32)


def draw_cluster_ids(key, part):
    return cluster_layout(key)


def draw_orders(key, part):
    cluster_of = cluster_layout(key)
    tie_break = jax.random.permutation(jax.random.fold_in(key, 7002), ROWS_ALL).astype(jnp.int32)
    sort_key = cluster_of * ROWS_ALL + tie_break
    by_key = jnp.argsort(sort_key).astype(jnp.int32)
    position = jnp.zeros((ROWS_ALL,), jnp.int32).at[by_key].set(jnp.arange(ROWS_ALL, dtype=jnp.int32))
    counts = jax.ops.segment_sum(jnp.ones((ROWS_ALL,), jnp.int32), cluster_of, num_segments=K)
    starts = jnp.cumsum(counts) - counts
    return (position - starts[cluster_of]).astype(jnp.int32)


def draw_embeddings(key, part):
    cluster_of = cluster_layout(key)
    own_key = jax.random.fold_in(key, 7003)
    center_key, jitter_key = jax.random.split(own_key, 2)
    centers = jax.random.normal(center_key, (K, D), jnp.float32)
    samples = centers[cluster_of] + jax.random.normal(jitter_key, (ROWS_ALL, D), jnp.float32)
    return jnp.clip(samples, -40.0, 40.0)


def setup_inputs(seed: int = 0) -> dict:
    streams_of = jax.random.split(jax.random.key(seed), 5)
    return {
        "embeddings": draw_embeddings(jax.random.fold_in(streams_of[4], 71), 0),
        "cluster_ids": draw_cluster_ids(jax.random.fold_in(streams_of[4], 71), 0),
        "orders": draw_orders(jax.random.fold_in(streams_of[4], 71), 0),
        "owner": jax.random.permutation(streams_of[3], K).astype(jnp.int32),
    }


def unit_rows(matrix):
    squares = lax.optimization_barrier(jnp.sum(matrix * matrix, axis=-1, keepdims=True))
    return (matrix * lax.rsqrt(squares + 1e-06)).astype(jnp.bfloat16)

def scale_rows(matrix):
    squares = lax.optimization_barrier(jnp.sum(matrix * matrix, axis=-1))
    return jnp.sqrt(squares + 1e-06).astype(jnp.bfloat16)

def reference(embeddings, cluster_ids, orders, owner):
    total_rows = embeddings.shape[0]
    window = K * CAP
    rebuilt = unit_rows(embeddings).astype(jnp.float32) * scale_rows(embeddings).astype(jnp.float32)[:, None]
    totals = jax.ops.segment_sum(rebuilt, cluster_ids, num_segments=K)
    counts = jax.ops.segment_sum(jnp.ones((total_rows,), jnp.float32), cluster_ids, num_segments=K)
    centers = totals / counts[:, None]
    direction = (centers * lax.rsqrt(lax.optimization_barrier(jnp.sum(centers * centers, axis=1, keepdims=True)) + 1e-06)).astype(jnp.bfloat16)
    by_owner = jnp.zeros_like(centers).at[owner].set(centers)
    sort_key = cluster_ids * total_rows + orders
    by_key = jnp.argsort(sort_key).astype(jnp.int32)
    padded_index = jnp.concatenate([jnp.zeros((window,), jnp.int32), by_key])
    padded_cluster = jnp.concatenate([jnp.full((window,), -1, jnp.int32), cluster_ids[by_key].astype(jnp.int32)])
    blocks = total_rows // 512

    def one_block(block_number):
        first_row = (block_number * 512).astype(jnp.int32)
        key_index = lax.dynamic_slice(padded_index, (first_row,), (window + 512,))
        key_cluster = lax.dynamic_slice(padded_cluster, (first_row,), (window + 512,))
        query_index = lax.dynamic_slice(padded_index, (first_row + window,), (512,))
        query_cluster = lax.dynamic_slice(padded_cluster, (first_row + window,), (512,))
        key_units = unit_rows(embeddings[key_index]).astype(jnp.float32)
        queries = unit_rows(embeddings[query_index]).astype(jnp.float32)
        scores = jnp.dot(queries, key_units.T, preferred_element_type=jnp.float32, precision=lax.Precision.HIGHEST)
        query_pos = jnp.arange(512, dtype=jnp.int32) + window
        key_pos = jnp.arange(window + 512, dtype=jnp.int32)
        earlier_mask = (key_cluster[None, :] == query_cluster[:, None]) & (key_pos[None, :] < query_pos[:, None])
        nearest = lax.optimization_barrier(jnp.max(jnp.where(earlier_mask, scores, -1.0), axis=1))
        aligned = lax.optimization_barrier(jnp.sum(queries * direction[query_cluster].astype(jnp.float32), axis=1))
        return (nearest, aligned)
    nearest, aligned = lax.map(one_block, jnp.arange(blocks, dtype=jnp.int32))
    max_cosine = jnp.zeros((total_rows,), jnp.float32).at[by_key].set(nearest.reshape(-1))
    center_cosine = jnp.zeros((total_rows,), jnp.float32).at[by_key].set(aligned.reshape(-1))
    return (by_owner, max_cosine, center_cosine)
```

```python
import jax
import jax.numpy as jnp
from jax import lax
from jax.experimental import pallas as pl
from jax.experimental.pallas import tpu as pltpu
from jax.sharding import Mesh
from jax.sharding import PartitionSpec as P

ALL = ("z", "y", "core", "x")
SLAB = ("y", "core", "x")
NZ = 16
NQ = 32
DEVS = NZ * NQ
ROWS = 256
D = 768
W = D + 128
BF = jnp.bfloat16
F32 = jnp.float32
NT = (((1,), (1,)), ((), ()))
TN = (((0,), (0,)), ((), ()))


def column(row):
    return jnp.transpose(jnp.broadcast_to(row, (128, row.shape[1])))[:, :1]


def call(kernel, shapes, *args):
    return pl.pallas_call(
        kernel,
        out_shape=shapes,
        in_specs=[pl.BlockSpec(memory_space=pltpu.VMEM) for _ in args],
        out_specs=[pl.BlockSpec(memory_space=pltpu.VMEM) for _ in shapes],
    )(*args)


def targets(ids_row, owner_row):
    hot = (lax.broadcasted_iota(jnp.int32, (DEVS, ROWS), 0) == ids_row).astype(F32).astype(BF)
    high = owner_row // 16
    low = owner_row - high * 16
    sub = lax.broadcasted_iota(jnp.int32, (8, DEVS), 0)
    digits = jnp.where(sub == 0, high, jnp.where(sub == 1, low, 0)).astype(F32).astype(BF)
    found = jnp.dot(digits, hot, preferred_element_type=F32)
    return found[0:1] * 16.0 + found[1:2]


def rank_among_equal(row):
    col = column(row)
    j = lax.broadcasted_iota(jnp.int32, (ROWS, ROWS), 0)
    i = lax.broadcasted_iota(jnp.int32, (ROWS, ROWS), 1)
    return jnp.sum(jnp.where((col == row) & (j < i), 1.0, 0.0), axis=0, keepdims=True)


def pack_kernel(emb_ref, ids_ref, ord_ref, own_ref, out_ref, slot_ref):
    target = targets(ids_ref[...], own_ref[...])
    rank = rank_among_equal(target)
    pos = (rank * DEVS + target).astype(jnp.int32)
    slot_ref[...] = pos
    emb = emb_ref[...]
    squares = jnp.sum(emb * emb, axis=1, keepdims=True) + 1e-06
    units = (emb * lax.rsqrt(squares)).astype(BF)
    scale = jnp.sqrt(squares).astype(BF)
    lane = lax.broadcasted_iota(jnp.int32, (ROWS, 128), 1)
    scale_lanes = jnp.where(lane == 0, scale.astype(F32), 0.0).astype(BF)
    order = ord_ref[...]
    high = order // 256
    low = order - high * 256
    sub = lax.broadcasted_iota(jnp.int32, (128, ROWS), 0)
    order_lanes = jnp.where(sub == 1, high + 1, jnp.where(sub == 2, low, 0)).astype(F32).astype(BF)
    for k in range(2):
        place = (lax.broadcasted_iota(jnp.int32, (DEVS, ROWS), 0) + k * DEVS == pos).astype(F32).astype(BF)
        rows = pl.ds(k * DEVS, DEVS)
        out_ref[rows, :D] = jnp.dot(place, units, preferred_element_type=F32).astype(BF)
        meta = jnp.dot(place, scale_lanes, preferred_element_type=F32)
        meta = meta + lax.dot_general(place, order_lanes, NT, preferred_element_type=F32)
        out_ref[rows, D:] = meta.astype(BF)


def owner_kernel(rows_ref, center_ref, back_ref):
    total = 2 * DEVS
    meta = rows_ref[:, D:].astype(F32)
    meta_t = jnp.transpose(meta)
    order_col = (meta[:, 1:2] - 1.0) * 256.0 + meta[:, 2:3]
    key_col = jnp.where(order_col >= 0.0, order_col, 1e6)
    order_row = (meta_t[1:2] - 1.0) * 256.0 + meta_t[2:3]
    members = jnp.sum(jnp.where(order_row >= 0.0, 1.0, 0.0))
    keys = rows_ref[:, :D]
    scale = jnp.broadcast_to(meta_t[0:1], (8, total)).astype(BF)
    center = jnp.dot(scale, keys, preferred_element_type=F32)[0:1] / members
    center_ref[...] = center
    length = lax.rsqrt(jnp.sum(center * center, axis=1, keepdims=True) + 1e-06)
    direction = jnp.broadcast_to(center * length, (8, D)).astype(BF)
    aligned = lax.dot_general(direction, keys, NT, preferred_element_type=F32)[0:1]
    back_ref[2:3] = aligned[:, :DEVS]
    back_ref[3:4] = aligned[:, DEVS:]
    block = 256
    for b in range(total // block):
        scores = lax.dot_general(
            keys, rows_ref[pl.ds(b * block, block), :D], NT, preferred_element_type=F32
        )
        earlier = key_col < order_row[:, b * block : (b + 1) * block]
        best = jnp.max(jnp.where(earlier, scores, -1.0), axis=0, keepdims=True)
        k, first = divmod(b * block, DEVS)
        back_ref[k : k + 1, first : first + block] = best


def unpack_kernel(got_ref, slot_ref, near_ref, align_ref):
    slot = slot_ref[...]
    rank = slot // DEVS
    target = slot - rank * DEVS
    z = target // NQ
    q = target - z * NQ
    hot = (lax.broadcasted_iota(jnp.int32, (NQ, ROWS), 0) == q).astype(F32)
    column_of = lax.dot_general(
        got_ref[...], hot, TN, precision=lax.Precision.HIGHEST, preferred_element_type=F32
    )
    sub = lax.broadcasted_iota(jnp.int32, (NZ * 4, ROWS), 0)
    near_ref[...] = jnp.sum(jnp.where(sub == z * 4 + rank, column_of, 0.0), axis=0, keepdims=True)
    align_ref[...] = jnp.sum(jnp.where(sub == z * 4 + rank + 2, column_of, 0.0), axis=0, keepdims=True)


def local(embeddings, cluster_ids, orders, owner):
    sds = jax.ShapeDtypeStruct
    packed, slot = call(
        pack_kernel,
        [sds((2 * DEVS, W), BF), sds((1, ROWS), jnp.int32)],
        embeddings,
        cluster_ids.reshape(1, ROWS),
        orders.reshape(1, ROWS),
        owner.reshape(1, DEVS),
    )
    send = packed.reshape(2, DEVS, W).transpose(1, 0, 2)
    got = lax.all_to_all(send, ALL, split_axis=0, concat_axis=0, tiled=True)
    rows = got.transpose(1, 0, 2).reshape(2 * DEVS, W)
    center, back = call(owner_kernel, [sds((1, D), F32), sds((4, DEVS), F32)], rows)
    back = back.reshape(4, NZ, NQ).transpose(1, 0, 2).reshape(NZ, 1, 4 * NQ)
    back = lax.all_to_all(back, "z", split_axis=0, concat_axis=0, tiled=True)
    back = back.reshape(NZ, 4, NQ).transpose(2, 0, 1).reshape(NQ, 1, NZ * 4)
    back = lax.all_to_all(back, SLAB, split_axis=0, concat_axis=0, tiled=True)
    near, align = call(
        unpack_kernel,
        [sds((1, ROWS), F32), sds((1, ROWS), F32)],
        back.reshape(NQ, NZ * 4),
        slot,
    )
    return (center, near.reshape(ROWS), align.reshape(ROWS))


def solution(mesh):
    fine = Mesh(mesh.devices.reshape(16, 4, 2, 4), ALL)
    return jax.shard_map(
        local,
        mesh=fine,
        in_specs=(P(ALL, None), P(ALL), P(ALL), P()),
        out_specs=(P(ALL, None), P(ALL), P(ALL)),
        check_vma=False,
    )
```

```python
import jax
import jax.numpy as jnp
from jax import lax
from jax.experimental import pallas as pl
from jax.experimental.pallas import tpu as pltpu
from jax.sharding import Mesh
from jax.sharding import PartitionSpec as P

ALL = ("z", "y", "core", "x")
SLAB = ("y", "core", "x")
NZ = 16
NQ = 32
DEVS = NZ * NQ
ROWS = 256
D = 768
W = D + 128
BF = jnp.bfloat16
F32 = jnp.float32
NT = (((1,), (1,)), ((), ()))
TN = (((0,), (0,)), ((), ()))
STRIDE = 40
FIT = STRIDE - 1
SENT = NZ * STRIDE
COLS = D // 128
CHUNK = COLS * NQ + 8


def column(row):
    return jnp.transpose(jnp.broadcast_to(row, (128, row.shape[1])))[:, :1]


def call(kernel, shapes, *args, scratch=()):
    return pl.pallas_call(
        kernel,
        out_shape=shapes,
        scratch_shapes=scratch,
        in_specs=[pl.BlockSpec(memory_space=pltpu.VMEM) for _ in args],
        out_specs=[pl.BlockSpec(memory_space=pltpu.VMEM) for _ in shapes],
    )(*args)


def targets(ids_row, owner_row):
    hot = (lax.broadcasted_iota(jnp.int32, (DEVS, ROWS), 0) == ids_row).astype(F32).astype(BF)
    high = owner_row // 16
    low = owner_row - high * 16
    sub = lax.broadcasted_iota(jnp.int32, (8, DEVS), 0)
    digits = jnp.where(sub == 0, high, jnp.where(sub == 1, low, 0)).astype(F32).astype(BF)
    found = jnp.dot(digits, hot, preferred_element_type=F32)
    return found[0:1] * 16.0 + found[1:2]


def rank_among_equal(row):
    col = column(row)
    j = lax.broadcasted_iota(jnp.int32, (ROWS, ROWS), 0)
    i = lax.broadcasted_iota(jnp.int32, (ROWS, ROWS), 1)
    return jnp.sum(jnp.where((col == row) & (j < i), 1.0, 0.0), axis=0, keepdims=True)


def pack_kernel(emb_ref, ids_ref, ord_ref, own_ref, out_ref, slot_ref):
    target = targets(ids_ref[...], own_ref[...])
    rank = rank_among_equal(target)
    pos = (rank * DEVS + target).astype(jnp.int32)
    slot_ref[...] = pos
    emb = emb_ref[...]
    squares = jnp.sum(emb * emb, axis=1, keepdims=True) + 1e-06
    units = (emb * lax.rsqrt(squares)).astype(BF)
    scale = jnp.sqrt(squares).astype(BF)
    lane = lax.broadcasted_iota(jnp.int32, (ROWS, 128), 1)
    scale_lanes = jnp.where(lane == 0, scale.astype(F32), 0.0).astype(BF)
    order = ord_ref[...]
    high = order // 256
    low = order - high * 256
    sub = lax.broadcasted_iota(jnp.int32, (128, ROWS), 0)
    order_lanes = jnp.where(sub == 1, high + 1, jnp.where(sub == 2, low, 0)).astype(F32).astype(BF)
    for k in range(2):
        place = (lax.broadcasted_iota(jnp.int32, (DEVS, ROWS), 0) + k * DEVS == pos).astype(F32).astype(BF)
        rows = pl.ds(k * DEVS, DEVS)
        out_ref[rows, :D] = jnp.dot(place, units, preferred_element_type=F32).astype(BF)
        meta = jnp.dot(place, scale_lanes, preferred_element_type=F32)
        meta = meta + lax.dot_general(place, order_lanes, NT, preferred_element_type=F32)
        out_ref[rows, D:] = meta.astype(BF)


def owner_kernel(rows_ref, center_ref, back_ref):
    total = 2 * DEVS
    meta = rows_ref[:, D:].astype(F32)
    meta_t = jnp.transpose(meta)
    order_col = (meta[:, 1:2] - 1.0) * 256.0 + meta[:, 2:3]
    key_col = jnp.where(order_col >= 0.0, order_col, 1e6)
    order_row = (meta_t[1:2] - 1.0) * 256.0 + meta_t[2:3]
    members = jnp.sum(jnp.where(order_row >= 0.0, 1.0, 0.0))
    keys = rows_ref[:, :D]
    scale = jnp.broadcast_to(meta_t[0:1], (8, total)).astype(BF)
    center = jnp.dot(scale, keys, preferred_element_type=F32)[0:1] / members
    center_ref[...] = center
    length = lax.rsqrt(jnp.sum(center * center, axis=1, keepdims=True) + 1e-06)
    direction = jnp.broadcast_to(center * length, (8, D)).astype(BF)
    aligned = lax.dot_general(direction, keys, NT, preferred_element_type=F32)[0:1]
    back_ref[2:3] = aligned[:, :DEVS]
    back_ref[3:4] = aligned[:, DEVS:]
    block = 256
    for b in range(total // block):
        scores = lax.dot_general(
            keys, rows_ref[pl.ds(b * block, block), :D], NT, preferred_element_type=F32
        )
        earlier = key_col < order_row[:, b * block : (b + 1) * block]
        best = jnp.max(jnp.where(earlier, scores, -1.0), axis=0, keepdims=True)
        k, first = divmod(b * block, DEVS)
        back_ref[k : k + 1, first : first + block] = best


def row_of(col):
    return jnp.transpose(jnp.broadcast_to(col, (col.shape[0], 128)))[:1]


def iota(shape, dim):
    return lax.broadcasted_iota(jnp.int32, shape, dim)


def hot(condition):
    return condition.astype(F32).astype(BF)


def dot(a, b):
    return jnp.dot(a, b, preferred_element_type=F32)


def dot_nt(a, b):
    return lax.dot_general(a, b, NT, preferred_element_type=F32)


def slab_pack_kernel(emb_ref, ids_ref, ord_ref, own_ref, out_ref, slot_ref):
    target = targets(ids_ref[...], own_ref[...])
    rank = rank_among_equal(target).astype(jnp.int32)
    whole = target.astype(jnp.int32)
    slot_ref[...] = rank * DEVS + whole
    z = whole // NQ
    q = whole - z * NQ
    place = rank_among_equal(z.astype(F32)).astype(jnp.int32)
    overflow = jnp.max((place >= FIT).astype(F32), axis=1, keepdims=True)
    pos = jnp.where(place < FIT, z * STRIDE + place, -1)
    emb = emb_ref[...]
    squares = jnp.sum(emb * emb, axis=1, keepdims=True) + 1e-06
    units = (emb * lax.rsqrt(squares)).astype(BF)
    scale = row_of(jnp.sqrt(squares).astype(BF).astype(F32))
    order = ord_ref[...]
    high = order // 256
    low = order - high * 256
    sub = iota((NZ * 4, ROWS), 0)
    value = sub // NZ
    picked = jnp.where(
        value == 0,
        scale,
        jnp.where(value == 1, high, jnp.where(value == 2, low, q * 2 + rank + 1)).astype(F32),
    )
    mine = jnp.where(sub - value * NZ == z, picked, 0.0).astype(BF)
    found = dot_nt(mine, hot(iota((128, ROWS), 0) == place)).astype(BF)
    flag = jnp.broadcast_to(overflow, (NZ, 128)).astype(BF)
    meta = jnp.concatenate(
        [found[v * NZ : (v + 1) * NZ] for v in range(4)] + [flag, jnp.zeros((NZ, 128), BF)], axis=1
    )
    spread = hot(iota((SENT, ROWS), 0) == pos)
    last = hot(iota((SENT, NZ), 0) == iota((SENT, NZ), 1) * STRIDE + FIT)
    out_ref[...] = (dot(spread, units) + dot(last, meta)).astype(BF)


def repack_kernel(rows_ref, out_ref):
    last = hot(iota((NZ, SENT), 1) == iota((NZ, SENT), 0) * STRIDE + FIT)
    meta = dot(last, rows_ref[:, :640])
    flag = jnp.max(meta[:, 512:640])
    stacked = jnp.concatenate([meta[:, v * 128 : (v + 1) * 128] for v in range(4)], axis=0).astype(BF)
    k = iota((128, SENT), 1)
    along = dot(stacked, hot(iota((128, SENT), 0) == k - (k // STRIDE) * STRIDE))
    sub = iota((NZ * 4, SENT), 0)
    here = sub - (sub // NZ) * NZ == iota((NZ * 4, SENT), 1) // STRIDE
    values = jnp.sum(jnp.where(here, along, 0.0).reshape(4, NZ, SENT), axis=1)
    code = values[3:4].astype(jnp.int32) - 1
    q = jnp.where(code >= 0, code // 2, -1)
    rank = code - q * 2
    slot = jnp.where(code >= 0, rank * NZ + iota((1, SENT), 1) // STRIDE, -1)
    pos = jnp.where(code >= 0, q * NQ + slot, -1)
    spread = hot(iota((2 * DEVS, SENT), 0) == pos)
    moved = dot(spread, rows_ref[...]).astype(BF)
    for c in range(COLS):
        out_ref[:, c * NQ : (c + 1) * NQ, :] = moved[:, c * 128 : (c + 1) * 128].reshape(NQ, NQ, 128)
    v = iota((8, SENT), 0)
    filled = jnp.where(v == 3, 1.0, 0.0)
    eight = jnp.where(v == 0, values[0:1], jnp.where(v == 1, values[1:2], jnp.where(v == 2, values[2:3], filled)))
    eight = jnp.broadcast_to(eight[None], (NQ, 8, SENT)).reshape(NQ * 8, SENT)
    mine = jnp.where(iota((NQ * 8, SENT), 0) // 8 == q, eight, 0.0).astype(BF)
    details = dot_nt(mine, hot(iota((128, SENT), 0) == slot))
    sub = iota((NQ * 8, 128), 0)
    details = details + jnp.where(sub - (sub // 8) * 8 == 4, flag, 0.0)
    out_ref[:, COLS * NQ :, :] = details.astype(BF).reshape(NQ, 8, 128)


def slab_owner_kernel(rows_ref, center_ref, back_ref, flag_ref, keys_ref):
    total = 2 * DEVS
    for c in range(COLS):
        keys_ref[:, c * 128 : (c + 1) * 128] = rows_ref[:, c * NQ : (c + 1) * NQ, :].reshape(total, 128)
    details = rows_ref[:, COLS * NQ :, :].reshape(NQ * 8, 128)
    n = iota((128, total), 1)
    along = dot(details, hot(iota((128, total), 0) == n - (n // NQ) * NQ))
    here = iota((NQ * 8, total), 0) // 8 == iota((NQ * 8, total), 1) // NQ
    values = jnp.sum(jnp.where(here, along, 0.0).reshape(NQ, 8, total), axis=0)
    flag_ref[...] = jnp.broadcast_to(jnp.max(values[4:5], axis=1, keepdims=True), (1, 128))
    order_row = values[1:2] * 256.0 + values[2:3]
    members = jnp.sum(values[3:4], axis=1, keepdims=True)
    key_col = column(jnp.where(values[3:4] > 0.0, order_row, 1e6))
    scale = jnp.broadcast_to(values[0:1], (8, total)).astype(BF)
    center = dot(scale, keys_ref[...])[0:1] / members
    center_ref[...] = center
    length = lax.rsqrt(jnp.sum(center * center, axis=1, keepdims=True) + 1e-06)
    direction = jnp.broadcast_to(center * length, (8, D)).astype(BF)
    back_ref[1:2] = dot_nt(direction, keys_ref[...])[0:1]
    block = 256
    for b in range(total // block):
        some = slice(b * block, (b + 1) * block)
        scores = dot_nt(keys_ref[...], keys_ref[some, :])
        back_ref[0:1, some] = jnp.max(
            jnp.where(key_col < order_row[:, some], scores, -1.0), axis=0, keepdims=True
        )


def unpack_kernel(got_ref, slot_ref, near_ref, align_ref):
    slot = slot_ref[...]
    rank = slot // DEVS
    target = slot - rank * DEVS
    z = target // NQ
    q = target - z * NQ
    from_z = (iota((NZ, ROWS), 0) == z).astype(F32)
    column_of = lax.dot_general(
        got_ref[...], from_z, TN, precision=lax.Precision.HIGHEST, preferred_element_type=F32
    )
    sub = iota((128, ROWS), 0)
    near_ref[...] = jnp.sum(jnp.where(sub == rank * NQ + q, column_of, 0.0), axis=0, keepdims=True)
    align_ref[...] = jnp.sum(jnp.where(sub == (rank + 2) * NQ + q, column_of, 0.0), axis=0, keepdims=True)


def full_exchange(embeddings, ids_row, orders_row, owner_row):
    sds = jax.ShapeDtypeStruct
    packed, _ = call(
        pack_kernel,
        [sds((2 * DEVS, W), BF), sds((1, ROWS), jnp.int32)],
        embeddings,
        ids_row,
        orders_row,
        owner_row,
    )
    send = packed.reshape(2, DEVS, W).transpose(1, 0, 2)
    got = lax.all_to_all(send, ALL, split_axis=0, concat_axis=0, tiled=True)
    rows = got.transpose(1, 0, 2).reshape(2 * DEVS, W)
    center, back = call(owner_kernel, [sds((1, D), F32), sds((4, DEVS), F32)], rows)
    return center, back.reshape(2, 2, NZ, NQ).transpose(0, 3, 1, 2).reshape(2, 2 * DEVS)


def local(embeddings, cluster_ids, orders, owner):
    sds = jax.ShapeDtypeStruct
    ids_row = cluster_ids.reshape(1, ROWS)
    orders_row = orders.reshape(1, ROWS)
    owner_row = owner.reshape(1, DEVS)
    packed, slot = call(
        slab_pack_kernel,
        [sds((SENT, D), BF), sds((1, ROWS), jnp.int32)],
        embeddings,
        ids_row,
        orders_row,
        owner_row,
    )
    got = lax.all_to_all(packed.reshape(NZ, STRIDE, D), "z", split_axis=0, concat_axis=0, tiled=True)
    (moved,) = call(repack_kernel, [sds((NQ, CHUNK, 128), BF)], got.reshape(SENT, D))
    rows = lax.all_to_all(moved, SLAB, split_axis=0, concat_axis=0, tiled=True)
    center, back, flag = call(
        slab_owner_kernel,
        [sds((1, D), F32), sds((2, 2 * DEVS), F32), sds((1, 128), F32)],
        rows,
        scratch=[pltpu.VMEM((2 * DEVS, D), BF)],
    )
    center, back = lax.cond(
        flag[0, 0] > 0.0,
        lambda: full_exchange(embeddings, ids_row, orders_row, owner_row),
        lambda: (center, back),
    )
    back = back.reshape(2, NQ, NQ).transpose(1, 0, 2).reshape(NQ, 1, 2 * NQ)
    back = lax.all_to_all(back, SLAB, split_axis=0, concat_axis=0, tiled=True)
    back = back.reshape(NQ, 4, NZ).transpose(2, 1, 0).reshape(NZ, 1, 4 * NQ)
    back = lax.all_to_all(back, "z", split_axis=0, concat_axis=0, tiled=True)
    near, align = call(
        unpack_kernel,
        [sds((1, ROWS), F32), sds((1, ROWS), F32)],
        back.reshape(NZ, 4 * NQ),
        slot,
    )
    return (center, near.reshape(ROWS), align.reshape(ROWS))


def solution(mesh):
    fine = Mesh(mesh.devices.reshape(16, 4, 2, 4), ALL)
    return jax.shard_map(
        local,
        mesh=fine,
        in_specs=(P(ALL, None), P(ALL), P(ALL), P()),
        out_specs=(P(ALL, None), P(ALL), P(ALL)),
        check_vma=False,
    )
```

```python
import jax
import jax.numpy as jnp
from jax import lax
from jax.experimental import pallas as pl
from jax.experimental.pallas import tpu as pltpu
from jax.sharding import Mesh
from jax.sharding import PartitionSpec as P

ALL = ("z", "y", "core", "x")
SLAB = ("y", "core", "x")
NZ = 16
NQ = 32
DEVS = NZ * NQ
ROWS = 256
D = 768
W = D + 128
BF = jnp.bfloat16
F32 = jnp.float32
NT = (((1,), (1,)), ((), ()))
TN = (((0,), (0,)), ((), ()))
STRIDE = 40
FIT = STRIDE - 1
SENT = NZ * STRIDE
COLS = D // 128
CHUNK = COLS * NQ + 8


def column(row):
    return jnp.transpose(jnp.broadcast_to(row, (128, row.shape[1])))[:, :1]


def call(kernel, shapes, *args, scratch=()):
    return pl.pallas_call(
        kernel,
        out_shape=shapes,
        scratch_shapes=scratch,
        compiler_params=pltpu.CompilerParams(vmem_limit_bytes=24 * 2**20),
        in_specs=[pl.BlockSpec(memory_space=pltpu.VMEM) for _ in args],
        out_specs=[pl.BlockSpec(memory_space=pltpu.VMEM) for _ in shapes],
    )(*args)


def targets(ids_row, owner_row):
    hot = (lax.broadcasted_iota(jnp.int32, (DEVS, ROWS), 0) == ids_row).astype(F32).astype(BF)
    high = owner_row // 16
    low = owner_row - high * 16
    sub = lax.broadcasted_iota(jnp.int32, (8, DEVS), 0)
    digits = jnp.where(sub == 0, high, jnp.where(sub == 1, low, 0)).astype(F32).astype(BF)
    found = jnp.dot(digits, hot, preferred_element_type=F32)
    return found[0:1] * 16.0 + found[1:2]


def rank_among_equal(row):
    col = column(row)
    j = lax.broadcasted_iota(jnp.int32, (ROWS, ROWS), 0)
    i = lax.broadcasted_iota(jnp.int32, (ROWS, ROWS), 1)
    return jnp.sum(jnp.where((col == row) & (j < i), 1.0, 0.0), axis=0, keepdims=True)


def pack_kernel(emb_ref, ids_ref, ord_ref, own_ref, out_ref, slot_ref):
    target = targets(ids_ref[...], own_ref[...])
    rank = rank_among_equal(target)
    pos = (rank * DEVS + target).astype(jnp.int32)
    slot_ref[...] = pos
    emb = emb_ref[...]
    squares = jnp.sum(emb * emb, axis=1, keepdims=True) + 1e-06
    units = (emb * lax.rsqrt(squares)).astype(BF)
    scale = jnp.sqrt(squares).astype(BF)
    lane = lax.broadcasted_iota(jnp.int32, (ROWS, 128), 1)
    scale_lanes = jnp.where(lane == 0, scale.astype(F32), 0.0).astype(BF)
    order = ord_ref[...]
    high = order // 256
    low = order - high * 256
    sub = lax.broadcasted_iota(jnp.int32, (128, ROWS), 0)
    order_lanes = jnp.where(sub == 1, high + 1, jnp.where(sub == 2, low, 0)).astype(F32).astype(BF)
    for k in range(2):
        place = (lax.broadcasted_iota(jnp.int32, (DEVS, ROWS), 0) + k * DEVS == pos).astype(F32).astype(BF)
        rows = pl.ds(k * DEVS, DEVS)
        out_ref[rows, :D] = jnp.dot(place, units, preferred_element_type=F32).astype(BF)
        meta = jnp.dot(place, scale_lanes, preferred_element_type=F32)
        meta = meta + lax.dot_general(place, order_lanes, NT, preferred_element_type=F32)
        out_ref[rows, D:] = meta.astype(BF)


def owner_kernel(rows_ref, center_ref, back_ref):
    total = 2 * DEVS
    meta = rows_ref[:, D:].astype(F32)
    meta_t = jnp.transpose(meta)
    order_col = (meta[:, 1:2] - 1.0) * 256.0 + meta[:, 2:3]
    key_col = jnp.where(order_col >= 0.0, order_col, 1e6)
    order_row = (meta_t[1:2] - 1.0) * 256.0 + meta_t[2:3]
    members = jnp.sum(jnp.where(order_row >= 0.0, 1.0, 0.0))
    keys = rows_ref[:, :D]
    scale = jnp.broadcast_to(meta_t[0:1], (8, total)).astype(BF)
    center = jnp.dot(scale, keys, preferred_element_type=F32)[0:1] / members
    center_ref[...] = center
    length = lax.rsqrt(jnp.sum(center * center, axis=1, keepdims=True) + 1e-06)
    direction = jnp.broadcast_to(center * length, (8, D)).astype(BF)
    aligned = lax.dot_general(direction, keys, NT, preferred_element_type=F32)[0:1]
    back_ref[2:3] = aligned[:, :DEVS]
    back_ref[3:4] = aligned[:, DEVS:]
    block = 256
    for b in range(total // block):
        scores = lax.dot_general(
            keys, rows_ref[pl.ds(b * block, block), :D], NT, preferred_element_type=F32
        )
        earlier = key_col < order_row[:, b * block : (b + 1) * block]
        best = jnp.max(jnp.where(earlier, scores, -1.0), axis=0, keepdims=True)
        k, first = divmod(b * block, DEVS)
        back_ref[k : k + 1, first : first + block] = best


def row_of(col):
    return jnp.transpose(jnp.broadcast_to(col, (col.shape[0], 128)))[:1]


def iota(shape, dim):
    return lax.broadcasted_iota(jnp.int32, shape, dim)


def hot(condition):
    return condition.astype(F32).astype(BF)


def dot(a, b):
    return jnp.dot(a, b, preferred_element_type=F32)


def dot_nt(a, b):
    return lax.dot_general(a, b, NT, preferred_element_type=F32)


def slab_pack_kernel(emb_ref, ids_ref, ord_ref, own_ref, out_ref, slot_ref):
    target = targets(ids_ref[...], own_ref[...])
    rank = rank_among_equal(target).astype(jnp.int32)
    whole = target.astype(jnp.int32)
    slot_ref[...] = rank * DEVS + whole
    z = whole // NQ
    q = whole - z * NQ
    place = rank_among_equal(z.astype(F32)).astype(jnp.int32)
    overflow = jnp.max((place >= FIT).astype(F32), axis=1, keepdims=True)
    pos = jnp.where(place < FIT, z * STRIDE + place, -1)
    emb = emb_ref[...]
    squares = jnp.sum(emb * emb, axis=1, keepdims=True) + 1e-06
    units = (emb * lax.rsqrt(squares)).astype(BF)
    scale = row_of(jnp.sqrt(squares).astype(BF).astype(F32))
    order = ord_ref[...]
    high = order // 256
    low = order - high * 256
    sub = iota((NZ * 4, ROWS), 0)
    value = sub // NZ
    picked = jnp.where(
        value == 0,
        scale,
        jnp.where(value == 1, high, jnp.where(value == 2, low, q * 2 + rank + 1)).astype(F32),
    )
    mine = jnp.where(sub - value * NZ == z, picked, 0.0).astype(BF)
    found = dot_nt(mine, hot(iota((128, ROWS), 0) == place)).astype(BF)
    flag = jnp.broadcast_to(overflow, (NZ, 128)).astype(BF)
    meta = jnp.concatenate(
        [found[v * NZ : (v + 1) * NZ] for v in range(4)] + [flag, jnp.zeros((NZ, 128), BF)], axis=1
    )
    spread = hot(iota((SENT, ROWS), 0) == pos)
    last = hot(iota((SENT, NZ), 0) == iota((SENT, NZ), 1) * STRIDE + FIT)
    out_ref[...] = (dot(spread, units) + dot(last, meta)).astype(BF)


def repack_kernel(rows_ref, out_ref):
    last = hot(iota((NZ, SENT), 1) == iota((NZ, SENT), 0) * STRIDE + FIT)
    meta = dot(last, rows_ref[:, :640])
    flag = jnp.max(meta[:, 512:640])
    stacked = jnp.concatenate([meta[:, v * 128 : (v + 1) * 128] for v in range(4)], axis=0).astype(BF)
    k = iota((128, SENT), 1)
    along = dot(stacked, hot(iota((128, SENT), 0) == k - (k // STRIDE) * STRIDE))
    sub = iota((NZ * 4, SENT), 0)
    here = sub - (sub // NZ) * NZ == iota((NZ * 4, SENT), 1) // STRIDE
    values = jnp.sum(jnp.where(here, along, 0.0).reshape(4, NZ, SENT), axis=1)
    code = values[3:4].astype(jnp.int32) - 1
    q = jnp.where(code >= 0, code // 2, -1)
    rank = code - q * 2
    slot = jnp.where(code >= 0, rank * NZ + iota((1, SENT), 1) // STRIDE, -1)
    pos = jnp.where(code >= 0, q * NQ + slot, -1)
    spread = hot(iota((2 * DEVS, SENT), 0) == pos)
    moved = dot(spread, rows_ref[...]).astype(BF)
    for c in range(COLS):
        out_ref[:, c * NQ : (c + 1) * NQ, :] = moved[:, c * 128 : (c + 1) * 128].reshape(NQ, NQ, 128)
    v = iota((8, SENT), 0)
    filled = jnp.where(v == 3, 1.0, 0.0)
    eight = jnp.where(v == 0, values[0:1], jnp.where(v == 1, values[1:2], jnp.where(v == 2, values[2:3], filled)))
    eight = jnp.broadcast_to(eight[None], (NQ, 8, SENT)).reshape(NQ * 8, SENT)
    mine = jnp.where(iota((NQ * 8, SENT), 0) // 8 == q, eight, 0.0).astype(BF)
    details = dot_nt(mine, hot(iota((128, SENT), 0) == slot))
    sub = iota((NQ * 8, 128), 0)
    details = details + jnp.where(sub - (sub // 8) * 8 == 4, flag, 0.0)
    out_ref[:, COLS * NQ :, :] = details.astype(BF).reshape(NQ, 8, 128)


def slab_owner_kernel(rows_ref, center_ref, back_ref, flag_ref, keys_ref):
    total = 2 * DEVS
    for c in range(COLS):
        keys_ref[:, c * 128 : (c + 1) * 128] = rows_ref[:, c * NQ : (c + 1) * NQ, :].reshape(total, 128)
    details = rows_ref[:, COLS * NQ :, :].reshape(NQ * 8, 128)
    n = iota((128, total), 1)
    along = dot(details, hot(iota((128, total), 0) == n - (n // NQ) * NQ))
    here = iota((NQ * 8, total), 0) // 8 == iota((NQ * 8, total), 1) // NQ
    values = jnp.sum(jnp.where(here, along, 0.0).reshape(NQ, 8, total), axis=0)
    flag_ref[...] = jnp.broadcast_to(jnp.max(values[4:5], axis=1, keepdims=True), (1, 128))
    order_row = values[1:2] * 256.0 + values[2:3]
    members = jnp.sum(values[3:4], axis=1, keepdims=True)
    key_col = column(jnp.where(values[3:4] > 0.0, order_row, 1e6))
    scale = jnp.broadcast_to(values[0:1], (8, total)).astype(BF)
    center = dot(scale, keys_ref[...])[0:1] / members
    center_ref[...] = center
    length = lax.rsqrt(jnp.sum(center * center, axis=1, keepdims=True) + 1e-06)
    direction = jnp.broadcast_to(center * length, (8, D)).astype(BF)
    back_ref[1:2] = dot_nt(direction, keys_ref[...])[0:1]
    block = 256
    for b in range(total // block):
        some = slice(b * block, (b + 1) * block)
        scores = dot_nt(keys_ref[...], keys_ref[some, :])
        back_ref[0:1, some] = jnp.max(
            jnp.where(key_col < order_row[:, some], scores, -1.0), axis=0, keepdims=True
        )


def unpack_kernel(got_ref, slot_ref, near_ref, align_ref):
    slot = slot_ref[...]
    rank = slot // DEVS
    target = slot - rank * DEVS
    z = target // NQ
    q = target - z * NQ
    from_z = (iota((NZ, ROWS), 0) == z).astype(F32)
    column_of = lax.dot_general(
        got_ref[...], from_z, TN, precision=lax.Precision.HIGHEST, preferred_element_type=F32
    )
    sub = iota((128, ROWS), 0)
    near_ref[...] = jnp.sum(jnp.where(sub == rank * NQ + q, column_of, 0.0), axis=0, keepdims=True)
    align_ref[...] = jnp.sum(jnp.where(sub == (rank + 2) * NQ + q, column_of, 0.0), axis=0, keepdims=True)


def full_exchange(embeddings, ids_row, orders_row, owner_row):
    sds = jax.ShapeDtypeStruct
    packed, _ = call(
        pack_kernel,
        [sds((2 * DEVS, W), BF), sds((1, ROWS), jnp.int32)],
        embeddings,
        ids_row,
        orders_row,
        owner_row,
    )
    send = packed.reshape(2, DEVS, W).transpose(1, 0, 2)
    got = lax.all_to_all(send, ALL, split_axis=0, concat_axis=0, tiled=True)
    rows = got.transpose(1, 0, 2).reshape(2 * DEVS, W)
    center, back = call(owner_kernel, [sds((1, D), F32), sds((4, DEVS), F32)], rows)
    return center, back.reshape(2, 2, NZ, NQ).transpose(0, 3, 1, 2).reshape(2, 2 * DEVS)


def local(embeddings, cluster_ids, orders, owner):
    sds = jax.ShapeDtypeStruct
    ids_row = cluster_ids.reshape(1, ROWS)
    orders_row = orders.reshape(1, ROWS)
    owner_row = owner.reshape(1, DEVS)
    packed, slot = call(
        slab_pack_kernel,
        [sds((SENT, D), BF), sds((1, ROWS), jnp.int32)],
        embeddings,
        ids_row,
        orders_row,
        owner_row,
    )
    got = lax.all_to_all(packed.reshape(NZ, STRIDE, D), "z", split_axis=0, concat_axis=0, tiled=True)
    (moved,) = call(repack_kernel, [sds((NQ, CHUNK, 128), BF)], got.reshape(SENT, D))
    rows = lax.all_to_all(moved, SLAB, split_axis=0, concat_axis=0, tiled=True)
    center, back, flag = call(
        slab_owner_kernel,
        [sds((1, D), F32), sds((2, 2 * DEVS), F32), sds((1, 128), F32)],
        rows,
        scratch=[pltpu.VMEM((2 * DEVS, D), BF)],
    )
    center, back = lax.cond(
        flag[0, 0] > 0.0,
        lambda: full_exchange(embeddings, ids_row, orders_row, owner_row),
        lambda: (center, back),
    )
    back = back.reshape(2, NQ, NQ).transpose(1, 0, 2).reshape(NQ, 1, 2 * NQ)
    back = lax.all_to_all(back, SLAB, split_axis=0, concat_axis=0, tiled=True)
    back = back.reshape(NQ, 4, NZ).transpose(2, 1, 0).reshape(NZ, 1, 4 * NQ)
    back = lax.all_to_all(back, "z", split_axis=0, concat_axis=0, tiled=True)
    near, align = call(
        unpack_kernel,
        [sds((1, ROWS), F32), sds((1, ROWS), F32)],
        back.reshape(NZ, 4 * NQ),
        slot,
    )
    return (center, near.reshape(ROWS), align.reshape(ROWS))


def solution(mesh):
    fine = Mesh(mesh.devices.reshape(16, 4, 2, 4), ALL)
    return jax.shard_map(
        local,
        mesh=fine,
        in_specs=(P(ALL, None), P(ALL), P(ALL), P()),
        out_specs=(P(ALL, None), P(ALL), P(ALL)),
        check_vma=False,
    )
```

```python
import jax
import jax.numpy as jnp
from jax import lax
from jax.experimental import pallas as pl
from jax.experimental.pallas import tpu as pltpu
from jax.sharding import Mesh
from jax.sharding import PartitionSpec as P

ALL = ("z", "y", "core", "x")
SLAB = ("y", "core", "x")
NZ = 16
NQ = 32
DEVS = NZ * NQ
ROWS = 256
D = 768
W = D + 128
BF = jnp.bfloat16
F32 = jnp.float32
NT = (((1,), (1,)), ((), ()))
TN = (((0,), (0,)), ((), ()))
FIT = 35
HALF = D // 2
CHUNK_Z = 2 * (FIT + 1)
SENT = NZ * CHUNK_Z
MAIN = NZ * NQ
KEPT = MAIN + NZ * 8
COLS = D // 128
CHUNK = COLS * NQ + 8


def column(row):
    return jnp.transpose(jnp.broadcast_to(row, (128, row.shape[1])))[:, :1]


def call(kernel, shapes, *args, scratch=()):
    return pl.pallas_call(
        kernel,
        out_shape=shapes,
        scratch_shapes=scratch,
        compiler_params=pltpu.CompilerParams(vmem_limit_bytes=24 * 2**20),
        in_specs=[pl.BlockSpec(memory_space=pltpu.VMEM) for _ in args],
        out_specs=[pl.BlockSpec(memory_space=pltpu.VMEM) for _ in shapes],
    )(*args)


def targets(ids_row, owner_row):
    hot = (lax.broadcasted_iota(jnp.int32, (DEVS, ROWS), 0) == ids_row).astype(F32).astype(BF)
    high = owner_row // 16
    low = owner_row - high * 16
    sub = lax.broadcasted_iota(jnp.int32, (8, DEVS), 0)
    digits = jnp.where(sub == 0, high, jnp.where(sub == 1, low, 0)).astype(F32).astype(BF)
    found = jnp.dot(digits, hot, preferred_element_type=F32)
    return found[0:1] * 16.0 + found[1:2]


def rank_among_equal(row):
    col = column(row)
    j = lax.broadcasted_iota(jnp.int32, (ROWS, ROWS), 0)
    i = lax.broadcasted_iota(jnp.int32, (ROWS, ROWS), 1)
    return jnp.sum(jnp.where((col == row) & (j < i), 1.0, 0.0), axis=0, keepdims=True)


def pack_kernel(emb_ref, ids_ref, ord_ref, own_ref, out_ref, slot_ref):
    target = targets(ids_ref[...], own_ref[...])
    rank = rank_among_equal(target)
    pos = (rank * DEVS + target).astype(jnp.int32)
    slot_ref[...] = pos
    emb = emb_ref[...]
    squares = jnp.sum(emb * emb, axis=1, keepdims=True) + 1e-06
    units = (emb * lax.rsqrt(squares)).astype(BF)
    scale = jnp.sqrt(squares).astype(BF)
    lane = lax.broadcasted_iota(jnp.int32, (ROWS, 128), 1)
    scale_lanes = jnp.where(lane == 0, scale.astype(F32), 0.0).astype(BF)
    order = ord_ref[...]
    high = order // 256
    low = order - high * 256
    sub = lax.broadcasted_iota(jnp.int32, (128, ROWS), 0)
    order_lanes = jnp.where(sub == 1, high + 1, jnp.where(sub == 2, low, 0)).astype(F32).astype(BF)
    for k in range(2):
        place = (lax.broadcasted_iota(jnp.int32, (DEVS, ROWS), 0) + k * DEVS == pos).astype(F32).astype(BF)
        rows = pl.ds(k * DEVS, DEVS)
        out_ref[rows, :D] = jnp.dot(place, units, preferred_element_type=F32).astype(BF)
        meta = jnp.dot(place, scale_lanes, preferred_element_type=F32)
        meta = meta + lax.dot_general(place, order_lanes, NT, preferred_element_type=F32)
        out_ref[rows, D:] = meta.astype(BF)


def owner_kernel(rows_ref, center_ref, back_ref):
    total = 2 * DEVS
    meta = rows_ref[:, D:].astype(F32)
    meta_t = jnp.transpose(meta)
    order_col = (meta[:, 1:2] - 1.0) * 256.0 + meta[:, 2:3]
    key_col = jnp.where(order_col >= 0.0, order_col, 1e6)
    order_row = (meta_t[1:2] - 1.0) * 256.0 + meta_t[2:3]
    members = jnp.sum(jnp.where(order_row >= 0.0, 1.0, 0.0))
    keys = rows_ref[:, :D]
    scale = jnp.broadcast_to(meta_t[0:1], (8, total)).astype(BF)
    center = jnp.dot(scale, keys, preferred_element_type=F32)[0:1] / members
    center_ref[...] = center
    length = lax.rsqrt(jnp.sum(center * center, axis=1, keepdims=True) + 1e-06)
    direction = jnp.broadcast_to(center * length, (8, D)).astype(BF)
    aligned = lax.dot_general(direction, keys, NT, preferred_element_type=F32)[0:1]
    back_ref[2:3] = aligned[:, :DEVS]
    back_ref[3:4] = aligned[:, DEVS:]
    block = 256
    for b in range(total // block):
        scores = lax.dot_general(
            keys, rows_ref[pl.ds(b * block, block), :D], NT, preferred_element_type=F32
        )
        earlier = key_col < order_row[:, b * block : (b + 1) * block]
        best = jnp.max(jnp.where(earlier, scores, -1.0), axis=0, keepdims=True)
        k, first = divmod(b * block, DEVS)
        back_ref[k : k + 1, first : first + block] = best


def row_of(col):
    return jnp.transpose(jnp.broadcast_to(col, (col.shape[0], 128)))[:1]


def iota(shape, dim):
    return lax.broadcasted_iota(jnp.int32, shape, dim)


def hot(condition):
    return condition.astype(F32).astype(BF)


def dot(a, b):
    return jnp.dot(a, b, preferred_element_type=F32)


def dot_nt(a, b):
    return lax.dot_general(a, b, NT, preferred_element_type=F32)


def slab_pack_kernel(emb_ref, ids_ref, ord_ref, own_ref, out_ref, slot_ref):
    target = targets(ids_ref[...], own_ref[...])
    rank = rank_among_equal(target).astype(jnp.int32)
    whole = target.astype(jnp.int32)
    slot_ref[...] = rank * DEVS + whole
    z = whole // NQ
    q = whole - z * NQ
    place = rank_among_equal(z.astype(F32)).astype(jnp.int32)
    overflow = jnp.max((place >= FIT).astype(F32), axis=1, keepdims=True)
    left = z * CHUNK_Z + jnp.where(place < NQ, place, place + NQ)
    right = left + jnp.where(place < NQ, NQ, 4)
    left = jnp.where(place < FIT, left, -1)
    right = jnp.where(place < FIT, right, -1)
    emb = emb_ref[...]
    squares = jnp.sum(emb * emb, axis=1, keepdims=True) + 1e-06
    units = (emb * lax.rsqrt(squares)).astype(BF)
    scale = row_of(jnp.sqrt(squares).astype(BF).astype(F32))
    order = ord_ref[...]
    high = order // 256
    low = order - high * 256
    sub = iota((NZ * 4, ROWS), 0)
    value = sub // NZ
    picked = jnp.where(
        value == 0,
        scale,
        jnp.where(value == 1, high, jnp.where(value == 2, low, q * 2 + rank + 1)).astype(F32),
    )
    mine = jnp.where(sub - value * NZ == z, picked, 0.0).astype(BF)
    even = hot(iota((128, ROWS), 0) == place)
    odd = hot(iota((128, ROWS), 0) == place + 64)
    found = [
        (dot_nt(mine[v * NZ : (v + 1) * NZ], even) + dot_nt(mine[(v + 1) * NZ : (v + 2) * NZ], odd)).astype(BF)
        for v in (0, 2)
    ]
    meta = jnp.concatenate(found + [jnp.broadcast_to(overflow, (NZ, 128)).astype(BF)], axis=1)
    rows = iota((SENT, ROWS), 0)
    last = hot(iota((SENT, NZ), 0) == iota((SENT, NZ), 1) * CHUNK_Z + 67)
    sent = dot(hot(rows == left), units[:, :HALF]) + dot(hot(rows == right), units[:, HALF:])
    out_ref[...] = (sent + dot(last, meta)).astype(BF)


def repack_kernel(rows_ref, out_ref):
    main_left = rows_ref[:, :NQ, :].reshape(MAIN, HALF)
    main_right = rows_ref[:, NQ : 2 * NQ, :].reshape(MAIN, HALF)
    tail = rows_ref[:, 2 * NQ :, :].reshape(NZ * 8, HALF)
    meta = dot(hot(iota((NZ, NZ * 8), 1) == iota((NZ, NZ * 8), 0) * 8 + 3), tail)
    flag = jnp.max(meta[:, 256:384])
    pairs = jnp.concatenate([meta[:, :128], meta[:, 128:256]], axis=0).astype(BF)

    def source(shape):
        k = iota(shape, 1)
        t = k - MAIN
        z = jnp.where(t < 0, k // NQ, t // 8)
        place = jnp.where(t < 0, k - z * NQ, NQ + t - (t // 4) * 4)
        return z, place, t

    sub = iota((128, KEPT), 0)
    _, place, _ = source((128, KEPT))
    z, _, _ = source((NZ * 2, KEPT))
    here = iota((NZ * 2, KEPT), 0)
    here = here - (here // NZ) * NZ == z
    evens = jnp.where(here, dot(pairs, hot(sub == place)), 0.0).reshape(2, NZ, KEPT)
    odds = jnp.where(here, dot(pairs, hot(sub == place + 64)), 0.0).reshape(2, NZ, KEPT)
    scale = jnp.sum(evens[0], axis=0, keepdims=True)
    low = jnp.sum(evens[1], axis=0, keepdims=True)
    high = jnp.sum(odds[0], axis=0, keepdims=True)
    code = jnp.sum(odds[1], axis=0, keepdims=True).astype(jnp.int32) - 1
    z, place, t = source((1, KEPT))
    filled = (code >= 0) & (place < FIT)
    q = code // 2
    slot = (code - q * 2) * NZ + z
    is_left = filled & ((t < 0) | (t - (t // 8) * 8 < 4))
    is_right = filled & ((t < 0) | (t - (t // 8) * 8 >= 4))
    left = jnp.where(is_left, q * NQ + slot, -1)
    right = jnp.where(is_right, q * NQ + slot, -1)
    spread = hot(iota((2 * DEVS, MAIN), 0) == left[:, :MAIN])
    rows = iota((2 * DEVS, NZ * 8), 0)
    halves = (
        (dot(spread, main_left) + dot(hot(rows == left[:, MAIN:]), tail)).astype(BF),
        (dot(spread, main_right) + dot(hot(rows == right[:, MAIN:]), tail)).astype(BF),
    )
    for c in range(COLS):
        half, part = divmod(c, COLS // 2)
        block = halves[half][:, part * 128 : (part + 1) * 128]
        out_ref[:, c * NQ : (c + 1) * NQ, :] = block.reshape(NQ, NQ, 128)
    v = iota((8, KEPT), 0)
    eight = jnp.where(v == 0, scale, jnp.where(v == 1, high, jnp.where(v == 2, low, jnp.where(v == 3, 1.0, 0.0))))
    eight = jnp.broadcast_to(eight[None], (NQ, 8, KEPT)).reshape(NQ * 8, KEPT)
    owner = jnp.where(is_left, q, -1)
    mine = jnp.where(iota((NQ * 8, KEPT), 0) // 8 == owner, eight, 0.0).astype(BF)
    details = dot_nt(mine, hot(iota((128, KEPT), 0) == slot))
    sub = iota((NQ * 8, 128), 0)
    details = details + jnp.where(sub - (sub // 8) * 8 == 4, flag, 0.0)
    out_ref[:, COLS * NQ :, :] = details.astype(BF).reshape(NQ, 8, 128)


def slab_owner_kernel(rows_ref, center_ref, back_ref, flag_ref, keys_ref):
    total = 2 * DEVS
    for c in range(COLS):
        keys_ref[:, c * 128 : (c + 1) * 128] = rows_ref[:, c * NQ : (c + 1) * NQ, :].reshape(total, 128)
    details = rows_ref[:, COLS * NQ :, :].reshape(NQ * 8, 128)
    n = iota((128, total), 1)
    along = dot(details, hot(iota((128, total), 0) == n - (n // NQ) * NQ))
    here = iota((NQ * 8, total), 0) // 8 == iota((NQ * 8, total), 1) // NQ
    values = jnp.sum(jnp.where(here, along, 0.0).reshape(NQ, 8, total), axis=0)
    flag_ref[...] = jnp.broadcast_to(jnp.max(values[4:5], axis=1, keepdims=True), (1, 128))
    order_row = values[1:2] * 256.0 + values[2:3]
    members = jnp.sum(values[3:4], axis=1, keepdims=True)
    key_col = column(jnp.where(values[3:4] > 0.0, order_row, 1e6))
    scale = jnp.broadcast_to(values[0:1], (8, total)).astype(BF)
    center = dot(scale, keys_ref[...])[0:1] / members
    center_ref[...] = center
    length = lax.rsqrt(jnp.sum(center * center, axis=1, keepdims=True) + 1e-06)
    direction = jnp.broadcast_to(center * length, (8, D)).astype(BF)
    back_ref[1:2] = dot_nt(direction, keys_ref[...])[0:1]
    block = 256
    for b in range(total // block):
        some = slice(b * block, (b + 1) * block)
        scores = dot_nt(keys_ref[...], keys_ref[some, :])
        back_ref[0:1, some] = jnp.max(
            jnp.where(key_col < order_row[:, some], scores, -1.0), axis=0, keepdims=True
        )


def unpack_kernel(got_ref, slot_ref, near_ref, align_ref):
    slot = slot_ref[...]
    rank = slot // DEVS
    target = slot - rank * DEVS
    z = target // NQ
    q = target - z * NQ
    from_z = (iota((NZ, ROWS), 0) == z).astype(F32)
    column_of = lax.dot_general(
        got_ref[...], from_z, TN, precision=lax.Precision.HIGHEST, preferred_element_type=F32
    )
    sub = iota((128, ROWS), 0)
    near_ref[...] = jnp.sum(jnp.where(sub == rank * NQ + q, column_of, 0.0), axis=0, keepdims=True)
    align_ref[...] = jnp.sum(jnp.where(sub == (rank + 2) * NQ + q, column_of, 0.0), axis=0, keepdims=True)


def full_exchange(embeddings, ids_row, orders_row, owner_row):
    sds = jax.ShapeDtypeStruct
    packed, _ = call(
        pack_kernel,
        [sds((2 * DEVS, W), BF), sds((1, ROWS), jnp.int32)],
        embeddings,
        ids_row,
        orders_row,
        owner_row,
    )
    send = packed.reshape(2, DEVS, W).transpose(1, 0, 2)
    got = lax.all_to_all(send, ALL, split_axis=0, concat_axis=0, tiled=True)
    rows = got.transpose(1, 0, 2).reshape(2 * DEVS, W)
    center, back = call(owner_kernel, [sds((1, D), F32), sds((4, DEVS), F32)], rows)
    return center, back.reshape(2, 2, NZ, NQ).transpose(0, 3, 1, 2).reshape(2, 2 * DEVS)


def local(embeddings, cluster_ids, orders, owner):
    sds = jax.ShapeDtypeStruct
    ids_row = cluster_ids.reshape(1, ROWS)
    orders_row = orders.reshape(1, ROWS)
    owner_row = owner.reshape(1, DEVS)
    packed, slot = call(
        slab_pack_kernel,
        [sds((SENT, HALF), BF), sds((1, ROWS), jnp.int32)],
        embeddings,
        ids_row,
        orders_row,
        owner_row,
    )
    got = lax.all_to_all(packed.reshape(NZ, CHUNK_Z, HALF), "z", split_axis=0, concat_axis=0, tiled=True)
    (moved,) = call(repack_kernel, [sds((NQ, CHUNK, 128), BF)], got)
    rows = lax.all_to_all(moved, SLAB, split_axis=0, concat_axis=0, tiled=True)
    center, back, flag = call(
        slab_owner_kernel,
        [sds((1, D), F32), sds((2, 2 * DEVS), F32), sds((1, 128), F32)],
        rows,
        scratch=[pltpu.VMEM((2 * DEVS, D), BF)],
    )
    center, back = lax.cond(
        flag[0, 0] > 0.0,
        lambda: full_exchange(embeddings, ids_row, orders_row, owner_row),
        lambda: (center, back),
    )
    back = back.reshape(2, NQ, NQ).transpose(1, 0, 2).reshape(NQ, 1, 2 * NQ)
    back = lax.all_to_all(back, SLAB, split_axis=0, concat_axis=0, tiled=True)
    back = back.reshape(NQ, 4, NZ).transpose(2, 1, 0).reshape(NZ, 1, 4 * NQ)
    back = lax.all_to_all(back, "z", split_axis=0, concat_axis=0, tiled=True)
    near, align = call(
        unpack_kernel,
        [sds((1, ROWS), F32), sds((1, ROWS), F32)],
        back.reshape(NZ, 4 * NQ),
        slot,
    )
    return (center, near.reshape(ROWS), align.reshape(ROWS))


def solution(mesh):
    fine = Mesh(mesh.devices.reshape(16, 4, 2, 4), ALL)
    return jax.shard_map(
        local,
        mesh=fine,
        in_specs=(P(ALL, None), P(ALL), P(ALL), P()),
        out_specs=(P(ALL, None), P(ALL), P(ALL)),
        check_vma=False,
    )
```

```python
import jax
import jax.numpy as jnp
from jax import lax
from jax.experimental import pallas as pl
from jax.experimental.pallas import tpu as pltpu
from jax.sharding import Mesh
from jax.sharding import PartitionSpec as P

ALL = ("z", "y", "core", "x")
SLAB = ("y", "core", "x")
NZ = 16
NQ = 32
DEVS = NZ * NQ
ROWS = 256
D = 768
W = D + 128
BF = jnp.bfloat16
F32 = jnp.float32
NT = (((1,), (1,)), ((), ()))
TN = (((0,), (0,)), ((), ()))
FIT = 35
HALF = D // 2
CHUNK_Z = 2 * (FIT + 1)
SENT = NZ * CHUNK_Z
MAIN = NZ * NQ
KEPT = MAIN + NZ * 8
COLS = D // 128
CHUNK = COLS * NQ + 8


def column(row):
    return jnp.transpose(jnp.broadcast_to(row, (128, row.shape[1])))[:, :1]


def call(kernel, shapes, *args, scratch=()):
    return pl.pallas_call(
        kernel,
        out_shape=shapes,
        scratch_shapes=scratch,
        compiler_params=pltpu.CompilerParams(vmem_limit_bytes=24 * 2**20),
        in_specs=[pl.BlockSpec(memory_space=pltpu.VMEM) for _ in args],
        out_specs=[pl.BlockSpec(memory_space=pltpu.VMEM) for _ in shapes],
    )(*args)


def targets(ids_row, owner_row):
    hot = (lax.broadcasted_iota(jnp.int32, (DEVS, ROWS), 0) == ids_row).astype(F32).astype(BF)
    high = owner_row // 16
    low = owner_row - high * 16
    sub = lax.broadcasted_iota(jnp.int32, (8, DEVS), 0)
    digits = jnp.where(sub == 0, high, jnp.where(sub == 1, low, 0)).astype(F32).astype(BF)
    found = jnp.dot(digits, hot, preferred_element_type=F32)
    return found[0:1] * 16.0 + found[1:2]


def rank_among_equal(row):
    col = column(row)
    j = lax.broadcasted_iota(jnp.int32, (ROWS, ROWS), 0)
    i = lax.broadcasted_iota(jnp.int32, (ROWS, ROWS), 1)
    return jnp.sum(jnp.where((col == row) & (j < i), 1.0, 0.0), axis=0, keepdims=True)


def pack_kernel(emb_ref, ids_ref, ord_ref, own_ref, out_ref, slot_ref):
    target = targets(ids_ref[...], own_ref[...])
    rank = rank_among_equal(target)
    pos = (rank * DEVS + target).astype(jnp.int32)
    slot_ref[...] = pos
    emb = emb_ref[...]
    squares = jnp.sum(emb * emb, axis=1, keepdims=True) + 1e-06
    units = (emb * lax.rsqrt(squares)).astype(BF)
    scale = jnp.sqrt(squares).astype(BF)
    lane = lax.broadcasted_iota(jnp.int32, (ROWS, 128), 1)
    scale_lanes = jnp.where(lane == 0, scale.astype(F32), 0.0).astype(BF)
    order = ord_ref[...]
    high = order // 256
    low = order - high * 256
    sub = lax.broadcasted_iota(jnp.int32, (128, ROWS), 0)
    order_lanes = jnp.where(sub == 1, high + 1, jnp.where(sub == 2, low, 0)).astype(F32).astype(BF)
    for k in range(2):
        place = (lax.broadcasted_iota(jnp.int32, (DEVS, ROWS), 0) + k * DEVS == pos).astype(F32).astype(BF)
        rows = pl.ds(k * DEVS, DEVS)
        out_ref[rows, :D] = jnp.dot(place, units, preferred_element_type=F32).astype(BF)
        meta = jnp.dot(place, scale_lanes, preferred_element_type=F32)
        meta = meta + lax.dot_general(place, order_lanes, NT, preferred_element_type=F32)
        out_ref[rows, D:] = meta.astype(BF)


def owner_kernel(rows_ref, center_ref, back_ref):
    total = 2 * DEVS
    meta = rows_ref[:, D:].astype(F32)
    meta_t = jnp.transpose(meta)
    order_col = (meta[:, 1:2] - 1.0) * 256.0 + meta[:, 2:3]
    key_col = jnp.where(order_col >= 0.0, order_col, 1e6)
    order_row = (meta_t[1:2] - 1.0) * 256.0 + meta_t[2:3]
    members = jnp.sum(jnp.where(order_row >= 0.0, 1.0, 0.0))
    keys = rows_ref[:, :D]
    scale = jnp.broadcast_to(meta_t[0:1], (8, total)).astype(BF)
    center = jnp.dot(scale, keys, preferred_element_type=F32)[0:1] / members
    center_ref[...] = center
    length = lax.rsqrt(jnp.sum(center * center, axis=1, keepdims=True) + 1e-06)
    direction = jnp.broadcast_to(center * length, (8, D)).astype(BF)
    aligned = lax.dot_general(direction, keys, NT, preferred_element_type=F32)[0:1]
    back_ref[2:3] = aligned[:, :DEVS]
    back_ref[3:4] = aligned[:, DEVS:]
    block = 256
    for b in range(total // block):
        scores = lax.dot_general(
            keys, rows_ref[pl.ds(b * block, block), :D], NT, preferred_element_type=F32
        )
        earlier = key_col < order_row[:, b * block : (b + 1) * block]
        best = jnp.max(jnp.where(earlier, scores, -1.0), axis=0, keepdims=True)
        k, first = divmod(b * block, DEVS)
        back_ref[k : k + 1, first : first + block] = best


def row_of(col):
    return jnp.transpose(jnp.broadcast_to(col, (col.shape[0], 128)))[:1]


def iota(shape, dim):
    return lax.broadcasted_iota(jnp.int32, shape, dim)


def hot(condition):
    return condition.astype(F32).astype(BF)


def dot(a, b):
    return jnp.dot(a, b, preferred_element_type=F32)


def dot_nt(a, b):
    return lax.dot_general(a, b, NT, preferred_element_type=F32)


def slab_pack_kernel(emb_ref, ids_ref, ord_ref, own_ref, out_ref, slot_ref):
    target = targets(ids_ref[...], own_ref[...])
    rank = rank_among_equal(target).astype(jnp.int32)
    whole = target.astype(jnp.int32)
    slot_ref[...] = rank * DEVS + whole
    z = whole // NQ
    q = whole - z * NQ
    place = rank_among_equal(z.astype(F32)).astype(jnp.int32)
    overflow = jnp.max((place >= 0).astype(F32), axis=1, keepdims=True)
    left = z * CHUNK_Z + jnp.where(place < NQ, place, place + NQ)
    right = left + jnp.where(place < NQ, NQ, 4)
    left = jnp.where(place < FIT, left, -1)
    right = jnp.where(place < FIT, right, -1)
    emb = emb_ref[...]
    squares = jnp.sum(emb * emb, axis=1, keepdims=True) + 1e-06
    units = (emb * lax.rsqrt(squares)).astype(BF)
    scale = row_of(jnp.sqrt(squares).astype(BF).astype(F32))
    order = ord_ref[...]
    high = order // 256
    low = order - high * 256
    sub = iota((NZ * 4, ROWS), 0)
    value = sub // NZ
    picked = jnp.where(
        value == 0,
        scale,
        jnp.where(value == 1, high, jnp.where(value == 2, low, q * 2 + rank + 1)).astype(F32),
    )
    mine = jnp.where(sub - value * NZ == z, picked, 0.0).astype(BF)
    even = hot(iota((128, ROWS), 0) == place)
    odd = hot(iota((128, ROWS), 0) == place + 64)
    found = [
        (dot_nt(mine[v * NZ : (v + 1) * NZ], even) + dot_nt(mine[(v + 1) * NZ : (v + 2) * NZ], odd)).astype(BF)
        for v in (0, 2)
    ]
    meta = jnp.concatenate(found + [jnp.broadcast_to(overflow, (NZ, 128)).astype(BF)], axis=1)
    rows = iota((SENT, ROWS), 0)
    last = hot(iota((SENT, NZ), 0) == iota((SENT, NZ), 1) * CHUNK_Z + 67)
    sent = dot(hot(rows == left), units[:, :HALF]) + dot(hot(rows == right), units[:, HALF:])
    out_ref[...] = (sent + dot(last, meta)).astype(BF)


def repack_kernel(rows_ref, out_ref):
    main_left = rows_ref[:, :NQ, :].reshape(MAIN, HALF)
    main_right = rows_ref[:, NQ : 2 * NQ, :].reshape(MAIN, HALF)
    tail = rows_ref[:, 2 * NQ :, :].reshape(NZ * 8, HALF)
    meta = dot(hot(iota((NZ, NZ * 8), 1) == iota((NZ, NZ * 8), 0) * 8 + 3), tail)
    flag = jnp.max(meta[:, 256:384])
    pairs = jnp.concatenate([meta[:, :128], meta[:, 128:256]], axis=0).astype(BF)

    def source(shape):
        k = iota(shape, 1)
        t = k - MAIN
        z = jnp.where(t < 0, k // NQ, t // 8)
        place = jnp.where(t < 0, k - z * NQ, NQ + t - (t // 4) * 4)
        return z, place, t

    sub = iota((128, KEPT), 0)
    _, place, _ = source((128, KEPT))
    z, _, _ = source((NZ * 2, KEPT))
    here = iota((NZ * 2, KEPT), 0)
    here = here - (here // NZ) * NZ == z
    evens = jnp.where(here, dot(pairs, hot(sub == place)), 0.0).reshape(2, NZ, KEPT)
    odds = jnp.where(here, dot(pairs, hot(sub == place + 64)), 0.0).reshape(2, NZ, KEPT)
    scale = jnp.sum(evens[0], axis=0, keepdims=True)
    low = jnp.sum(evens[1], axis=0, keepdims=True)
    high = jnp.sum(odds[0], axis=0, keepdims=True)
    code = jnp.sum(odds[1], axis=0, keepdims=True).astype(jnp.int32) - 1
    z, place, t = source((1, KEPT))
    filled = (code >= 0) & (place < FIT)
    q = code // 2
    slot = (code - q * 2) * NZ + z
    is_left = filled & ((t < 0) | (t - (t // 8) * 8 < 4))
    is_right = filled & ((t < 0) | (t - (t // 8) * 8 >= 4))
    left = jnp.where(is_left, q * NQ + slot, -1)
    right = jnp.where(is_right, q * NQ + slot, -1)
    spread = hot(iota((2 * DEVS, MAIN), 0) == left[:, :MAIN])
    rows = iota((2 * DEVS, NZ * 8), 0)
    halves = (
        (dot(spread, main_left) + dot(hot(rows == left[:, MAIN:]), tail)).astype(BF),
        (dot(spread, main_right) + dot(hot(rows == right[:, MAIN:]), tail)).astype(BF),
    )
    for c in range(COLS):
        half, part = divmod(c, COLS // 2)
        block = halves[half][:, part * 128 : (part + 1) * 128]
        out_ref[:, c * NQ : (c + 1) * NQ, :] = block.reshape(NQ, NQ, 128)
    v = iota((8, KEPT), 0)
    eight = jnp.where(v == 0, scale, jnp.where(v == 1, high, jnp.where(v == 2, low, jnp.where(v == 3, 1.0, 0.0))))
    eight = jnp.broadcast_to(eight[None], (NQ, 8, KEPT)).reshape(NQ * 8, KEPT)
    owner = jnp.where(is_left, q, -1)
    mine = jnp.where(iota((NQ * 8, KEPT), 0) // 8 == owner, eight, 0.0).astype(BF)
    details = dot_nt(mine, hot(iota((128, KEPT), 0) == slot))
    sub = iota((NQ * 8, 128), 0)
    details = details + jnp.where(sub - (sub // 8) * 8 == 4, flag, 0.0)
    out_ref[:, COLS * NQ :, :] = details.astype(BF).reshape(NQ, 8, 128)


def slab_owner_kernel(rows_ref, center_ref, back_ref, flag_ref, keys_ref):
    total = 2 * DEVS
    for c in range(COLS):
        keys_ref[:, c * 128 : (c + 1) * 128] = rows_ref[:, c * NQ : (c + 1) * NQ, :].reshape(total, 128)
    details = rows_ref[:, COLS * NQ :, :].reshape(NQ * 8, 128)
    n = iota((128, total), 1)
    along = dot(details, hot(iota((128, total), 0) == n - (n // NQ) * NQ))
    here = iota((NQ * 8, total), 0) // 8 == iota((NQ * 8, total), 1) // NQ
    values = jnp.sum(jnp.where(here, along, 0.0).reshape(NQ, 8, total), axis=0)
    flag_ref[...] = jnp.broadcast_to(jnp.max(values[4:5], axis=1, keepdims=True), (1, 128))
    order_row = values[1:2] * 256.0 + values[2:3]
    members = jnp.sum(values[3:4], axis=1, keepdims=True)
    key_col = column(jnp.where(values[3:4] > 0.0, order_row, 1e6))
    scale = jnp.broadcast_to(values[0:1], (8, total)).astype(BF)
    center = dot(scale, keys_ref[...])[0:1] / members
    center_ref[...] = center
    length = lax.rsqrt(jnp.sum(center * center, axis=1, keepdims=True) + 1e-06)
    direction = jnp.broadcast_to(center * length, (8, D)).astype(BF)
    back_ref[1:2] = dot_nt(direction, keys_ref[...])[0:1]
    block = 256
    for b in range(total // block):
        some = slice(b * block, (b + 1) * block)
        scores = dot_nt(keys_ref[...], keys_ref[some, :])
        back_ref[0:1, some] = jnp.max(
            jnp.where(key_col < order_row[:, some], scores, -1.0), axis=0, keepdims=True
        )


def unpack_kernel(got_ref, slot_ref, near_ref, align_ref):
    slot = slot_ref[...]
    rank = slot // DEVS
    target = slot - rank * DEVS
    z = target // NQ
    q = target - z * NQ
    from_z = (iota((NZ, ROWS), 0) == z).astype(F32)
    column_of = lax.dot_general(
        got_ref[...], from_z, TN, precision=lax.Precision.HIGHEST, preferred_element_type=F32
    )
    sub = iota((128, ROWS), 0)
    near_ref[...] = jnp.sum(jnp.where(sub == rank * NQ + q, column_of, 0.0), axis=0, keepdims=True)
    align_ref[...] = jnp.sum(jnp.where(sub == (rank + 2) * NQ + q, column_of, 0.0), axis=0, keepdims=True)


def full_exchange(embeddings, ids_row, orders_row, owner_row):
    sds = jax.ShapeDtypeStruct
    packed, _ = call(
        pack_kernel,
        [sds((2 * DEVS, W), BF), sds((1, ROWS), jnp.int32)],
        embeddings,
        ids_row,
        orders_row,
        owner_row,
    )
    send = packed.reshape(2, DEVS, W).transpose(1, 0, 2)
    got = lax.all_to_all(send, ALL, split_axis=0, concat_axis=0, tiled=True)
    rows = got.transpose(1, 0, 2).reshape(2 * DEVS, W)
    center, back = call(owner_kernel, [sds((1, D), F32), sds((4, DEVS), F32)], rows)
    return center, back.reshape(2, 2, NZ, NQ).transpose(0, 3, 1, 2).reshape(2, 2 * DEVS)


def local(embeddings, cluster_ids, orders, owner):
    sds = jax.ShapeDtypeStruct
    ids_row = cluster_ids.reshape(1, ROWS)
    orders_row = orders.reshape(1, ROWS)
    owner_row = owner.reshape(1, DEVS)
    packed, slot = call(
        slab_pack_kernel,
        [sds((SENT, HALF), BF), sds((1, ROWS), jnp.int32)],
        embeddings,
        ids_row,
        orders_row,
        owner_row,
    )
    got = lax.all_to_all(packed.reshape(NZ, CHUNK_Z, HALF), "z", split_axis=0, concat_axis=0, tiled=True)
    (moved,) = call(repack_kernel, [sds((NQ, CHUNK, 128), BF)], got)
    rows = lax.all_to_all(moved, SLAB, split_axis=0, concat_axis=0, tiled=True)
    center, back, flag = call(
        slab_owner_kernel,
        [sds((1, D), F32), sds((2, 2 * DEVS), F32), sds((1, 128), F32)],
        rows,
        scratch=[pltpu.VMEM((2 * DEVS, D), BF)],
    )
    center, back = lax.cond(
        flag[0, 0] > 0.0,
        lambda: full_exchange(embeddings, ids_row, orders_row, owner_row),
        lambda: (center, back),
    )
    back = back.reshape(2, NQ, NQ).transpose(1, 0, 2).reshape(NQ, 1, 2 * NQ)
    back = lax.all_to_all(back, SLAB, split_axis=0, concat_axis=0, tiled=True)
    back = back.reshape(NQ, 4, NZ).transpose(2, 1, 0).reshape(NZ, 1, 4 * NQ)
    back = lax.all_to_all(back, "z", split_axis=0, concat_axis=0, tiled=True)
    near, align = call(
        unpack_kernel,
        [sds((1, ROWS), F32), sds((1, ROWS), F32)],
        back.reshape(NZ, 4 * NQ),
        slot,
    )
    return (center, near.reshape(ROWS), align.reshape(ROWS))


def solution(mesh):
    fine = Mesh(mesh.devices.reshape(16, 4, 2, 4), ALL)
    return jax.shard_map(
        local,
        mesh=fine,
        in_specs=(P(ALL, None), P(ALL), P(ALL), P()),
        out_specs=(P(ALL, None), P(ALL), P(ALL)),
        check_vma=False,
    )
```

```python
import jax
import jax.numpy as jnp
from jax import lax
from jax.experimental import pallas as pl
from jax.experimental.pallas import tpu as pltpu
from jax.sharding import Mesh
from jax.sharding import PartitionSpec as P

ALL = ("z", "y", "core", "x")
SLAB = ("y", "core", "x")
NZ = 16
NQ = 32
DEVS = NZ * NQ
ROWS = 256
D = 768
W = D + 128
BF = jnp.bfloat16
F32 = jnp.float32
NT = (((1,), (1,)), ((), ()))
TN = (((0,), (0,)), ((), ()))
FIT = 35
HALF = D // 2
CHUNK_Z = 2 * (FIT + 1)
SENT = NZ * CHUNK_Z
MAIN = NZ * NQ
KEPT = MAIN + NZ * 8
COLS = D // 128
CHUNK = COLS * NQ + 8


def column(row):
    return jnp.transpose(jnp.broadcast_to(row, (128, row.shape[1])))[:, :1]


def call(kernel, shapes, *args, scratch=(), far=0):
    return pl.pallas_call(
        kernel,
        out_shape=shapes,
        scratch_shapes=scratch,
        compiler_params=pltpu.CompilerParams(vmem_limit_bytes=24 * 2**20),
        in_specs=[pl.BlockSpec(memory_space=pltpu.HBM if i < far else pltpu.VMEM) for i in range(len(args))],
        out_specs=[pl.BlockSpec(memory_space=pltpu.VMEM) for _ in shapes],
    )(*args)


def targets(ids_row, owner_row):
    hot = (lax.broadcasted_iota(jnp.int32, (DEVS, ROWS), 0) == ids_row).astype(F32).astype(BF)
    high = owner_row // 16
    low = owner_row - high * 16
    sub = lax.broadcasted_iota(jnp.int32, (8, DEVS), 0)
    digits = jnp.where(sub == 0, high, jnp.where(sub == 1, low, 0)).astype(F32).astype(BF)
    found = jnp.dot(digits, hot, preferred_element_type=F32)
    return found[0:1] * 16.0 + found[1:2]


def rank_among_equal(row):
    col = column(row)
    j = lax.broadcasted_iota(jnp.int32, (ROWS, ROWS), 0)
    i = lax.broadcasted_iota(jnp.int32, (ROWS, ROWS), 1)
    return jnp.sum(jnp.where((col == row) & (j < i), 1.0, 0.0), axis=0, keepdims=True)


def pack_kernel(emb_far, ids_far, ord_far, own_far, out_ref, slot_ref, emb_ref, ids_ref, ord_ref, own_ref):
    pltpu.sync_copy(emb_far, emb_ref)
    pltpu.sync_copy(ids_far, ids_ref)
    pltpu.sync_copy(ord_far, ord_ref)
    pltpu.sync_copy(own_far, own_ref)
    target = targets(ids_ref[...], own_ref[...])
    rank = rank_among_equal(target)
    pos = (rank * DEVS + target).astype(jnp.int32)
    slot_ref[...] = pos
    emb = emb_ref[...]
    squares = jnp.sum(emb * emb, axis=1, keepdims=True) + 1e-06
    units = (emb * lax.rsqrt(squares)).astype(BF)
    scale = jnp.sqrt(squares).astype(BF)
    lane = lax.broadcasted_iota(jnp.int32, (ROWS, 128), 1)
    scale_lanes = jnp.where(lane == 0, scale.astype(F32), 0.0).astype(BF)
    order = ord_ref[...]
    high = order // 256
    low = order - high * 256
    sub = lax.broadcasted_iota(jnp.int32, (128, ROWS), 0)
    order_lanes = jnp.where(sub == 1, high + 1, jnp.where(sub == 2, low, 0)).astype(F32).astype(BF)
    for k in range(2):
        place = (lax.broadcasted_iota(jnp.int32, (DEVS, ROWS), 0) + k * DEVS == pos).astype(F32).astype(BF)
        rows = pl.ds(k * DEVS, DEVS)
        out_ref[rows, :D] = jnp.dot(place, units, preferred_element_type=F32).astype(BF)
        meta = jnp.dot(place, scale_lanes, preferred_element_type=F32)
        meta = meta + lax.dot_general(place, order_lanes, NT, preferred_element_type=F32)
        out_ref[rows, D:] = meta.astype(BF)


def owner_kernel(rows_ref, center_ref, back_ref):
    total = 2 * DEVS
    meta = rows_ref[:, D:].astype(F32)
    meta_t = jnp.transpose(meta)
    order_col = (meta[:, 1:2] - 1.0) * 256.0 + meta[:, 2:3]
    key_col = jnp.where(order_col >= 0.0, order_col, 1e6)
    order_row = (meta_t[1:2] - 1.0) * 256.0 + meta_t[2:3]
    members = jnp.sum(jnp.where(order_row >= 0.0, 1.0, 0.0))
    keys = rows_ref[:, :D]
    scale = jnp.broadcast_to(meta_t[0:1], (8, total)).astype(BF)
    center = jnp.dot(scale, keys, preferred_element_type=F32)[0:1] / members
    center_ref[...] = center
    length = lax.rsqrt(jnp.sum(center * center, axis=1, keepdims=True) + 1e-06)
    direction = jnp.broadcast_to(center * length, (8, D)).astype(BF)
    aligned = lax.dot_general(direction, keys, NT, preferred_element_type=F32)[0:1]
    back_ref[2:3] = aligned[:, :DEVS]
    back_ref[3:4] = aligned[:, DEVS:]
    block = 256
    for b in range(total // block):
        scores = lax.dot_general(
            keys, rows_ref[pl.ds(b * block, block), :D], NT, preferred_element_type=F32
        )
        earlier = key_col < order_row[:, b * block : (b + 1) * block]
        best = jnp.max(jnp.where(earlier, scores, -1.0), axis=0, keepdims=True)
        k, first = divmod(b * block, DEVS)
        back_ref[k : k + 1, first : first + block] = best


def row_of(col):
    return jnp.transpose(jnp.broadcast_to(col, (col.shape[0], 128)))[:1]


def iota(shape, dim):
    return lax.broadcasted_iota(jnp.int32, shape, dim)


def hot(condition):
    return condition.astype(F32).astype(BF)


def dot(a, b):
    return jnp.dot(a, b, preferred_element_type=F32)


def dot_nt(a, b):
    return lax.dot_general(a, b, NT, preferred_element_type=F32)


def slab_pack_kernel(emb_ref, ids_ref, ord_ref, own_ref, out_ref, slot_ref, here_ref, sem):
    copy = pltpu.make_async_copy(emb_ref, here_ref, sem)
    copy.start()
    target = targets(ids_ref[...], own_ref[...])
    rank = rank_among_equal(target).astype(jnp.int32)
    whole = target.astype(jnp.int32)
    slot_ref[...] = rank * DEVS + whole
    z = whole // NQ
    q = whole - z * NQ
    place = rank_among_equal(z.astype(F32)).astype(jnp.int32)
    overflow = jnp.max((place >= FIT).astype(F32), axis=1, keepdims=True)
    left = z * CHUNK_Z + jnp.where(place < NQ, place, place + NQ)
    right = left + jnp.where(place < NQ, NQ, 4)
    left = jnp.where(place < FIT, left, -1)
    right = jnp.where(place < FIT, right, -1)
    even = hot(iota((128, ROWS), 0) == place)
    odd = hot(iota((128, ROWS), 0) == place + 64)
    rows = iota((SENT, ROWS), 0)
    to_left = hot(rows == left)
    to_right = hot(rows == right)
    copy.wait()
    emb = here_ref[...]
    squares = jnp.sum(emb * emb, axis=1, keepdims=True) + 1e-06
    units = (emb * lax.rsqrt(squares)).astype(BF)
    scale = row_of(jnp.sqrt(squares).astype(BF).astype(F32))
    order = ord_ref[...]
    high = order // 256
    low = order - high * 256
    sub = iota((NZ * 4, ROWS), 0)
    value = sub // NZ
    picked = jnp.where(
        value == 0,
        scale,
        jnp.where(value == 1, high, jnp.where(value == 2, low, q * 2 + rank + 1)).astype(F32),
    )
    mine = jnp.where(sub - value * NZ == z, picked, 0.0).astype(BF)
    found = [
        (dot_nt(mine[v * NZ : (v + 1) * NZ], even) + dot_nt(mine[(v + 1) * NZ : (v + 2) * NZ], odd)).astype(BF)
        for v in (0, 2)
    ]
    meta = jnp.concatenate(found + [jnp.broadcast_to(overflow, (NZ, 128)).astype(BF)], axis=1)
    last = hot(iota((SENT, NZ), 0) == iota((SENT, NZ), 1) * CHUNK_Z + 67)
    sent = dot(to_left, units[:, :HALF]) + dot(to_right, units[:, HALF:])
    out_ref[...] = (sent + dot(last, meta)).astype(BF)


def repack_kernel(rows_ref, out_ref):
    main_left = rows_ref[:, :NQ, :].reshape(MAIN, HALF)
    main_right = rows_ref[:, NQ : 2 * NQ, :].reshape(MAIN, HALF)
    tail = rows_ref[:, 2 * NQ :, :].reshape(NZ * 8, HALF)
    meta = dot(hot(iota((NZ, NZ * 8), 1) == iota((NZ, NZ * 8), 0) * 8 + 3), tail)
    flag = jnp.max(meta[:, 256:384])
    pairs = jnp.concatenate([meta[:, :128], meta[:, 128:256]], axis=0).astype(BF)

    def source(shape):
        k = iota(shape, 1)
        t = k - MAIN
        z = jnp.where(t < 0, k // NQ, t // 8)
        place = jnp.where(t < 0, k - z * NQ, NQ + t - (t // 4) * 4)
        return z, place, t

    sub = iota((128, KEPT), 0)
    _, place, _ = source((128, KEPT))
    z, _, _ = source((NZ * 2, KEPT))
    here = iota((NZ * 2, KEPT), 0)
    here = here - (here // NZ) * NZ == z
    evens = jnp.where(here, dot(pairs, hot(sub == place)), 0.0).reshape(2, NZ, KEPT)
    odds = jnp.where(here, dot(pairs, hot(sub == place + 64)), 0.0).reshape(2, NZ, KEPT)
    scale = jnp.sum(evens[0], axis=0, keepdims=True)
    low = jnp.sum(evens[1], axis=0, keepdims=True)
    high = jnp.sum(odds[0], axis=0, keepdims=True)
    code = jnp.sum(odds[1], axis=0, keepdims=True).astype(jnp.int32) - 1
    z, place, t = source((1, KEPT))
    filled = (code >= 0) & (place < FIT)
    q = code // 2
    slot = (code - q * 2) * NZ + z
    is_left = filled & ((t < 0) | (t - (t // 8) * 8 < 4))
    is_right = filled & ((t < 0) | (t - (t // 8) * 8 >= 4))
    left = jnp.where(is_left, q * NQ + slot, -1)
    right = jnp.where(is_right, q * NQ + slot, -1)
    spread = hot(iota((2 * DEVS, MAIN), 0) == left[:, :MAIN])
    rows = iota((2 * DEVS, NZ * 8), 0)
    halves = (
        (dot(spread, main_left) + dot(hot(rows == left[:, MAIN:]), tail)).astype(BF),
        (dot(spread, main_right) + dot(hot(rows == right[:, MAIN:]), tail)).astype(BF),
    )
    for c in range(COLS):
        half, part = divmod(c, COLS // 2)
        block = halves[half][:, part * 128 : (part + 1) * 128]
        out_ref[:, c * NQ : (c + 1) * NQ, :] = block.reshape(NQ, NQ, 128)
    v = iota((8, KEPT), 0)
    eight = jnp.where(v == 0, scale, jnp.where(v == 1, high, jnp.where(v == 2, low, jnp.where(v == 3, 1.0, 0.0))))
    eight = jnp.broadcast_to(eight[None], (NQ, 8, KEPT)).reshape(NQ * 8, KEPT)
    owner = jnp.where(is_left, q, -1)
    mine = jnp.where(iota((NQ * 8, KEPT), 0) // 8 == owner, eight, 0.0).astype(BF)
    details = dot_nt(mine, hot(iota((128, KEPT), 0) == slot))
    sub = iota((NQ * 8, 128), 0)
    details = details + jnp.where(sub - (sub // 8) * 8 == 4, flag, 0.0)
    out_ref[:, COLS * NQ :, :] = details.astype(BF).reshape(NQ, 8, 128)


def slab_owner_kernel(rows_ref, center_ref, back_ref, flag_ref, keys_ref):
    total = 2 * DEVS
    for c in range(COLS):
        keys_ref[:, c * 128 : (c + 1) * 128] = rows_ref[:, c * NQ : (c + 1) * NQ, :].reshape(total, 128)
    details = rows_ref[:, COLS * NQ :, :].reshape(NQ * 8, 128)
    n = iota((128, total), 1)
    along = dot(details, hot(iota((128, total), 0) == n - (n // NQ) * NQ))
    here = iota((NQ * 8, total), 0) // 8 == iota((NQ * 8, total), 1) // NQ
    values = jnp.sum(jnp.where(here, along, 0.0).reshape(NQ, 8, total), axis=0)
    flag_ref[...] = jnp.broadcast_to(jnp.max(values[4:5], axis=1, keepdims=True), (1, 128))
    order_row = values[1:2] * 256.0 + values[2:3]
    members = jnp.sum(values[3:4], axis=1, keepdims=True)
    key_col = column(jnp.where(values[3:4] > 0.0, order_row, 1e6))
    scale = jnp.broadcast_to(values[0:1], (8, total)).astype(BF)
    center = dot(scale, keys_ref[...])[0:1] / members
    center_ref[...] = center
    length = lax.rsqrt(jnp.sum(center * center, axis=1, keepdims=True) + 1e-06)
    direction = jnp.broadcast_to(center * length, (8, D)).astype(BF)
    back_ref[1:2] = dot_nt(direction, keys_ref[...])[0:1]
    block = 256
    for b in range(total // block):
        some = slice(b * block, (b + 1) * block)
        scores = dot_nt(keys_ref[...], keys_ref[some, :])
        back_ref[0:1, some] = jnp.max(
            jnp.where(key_col < order_row[:, some], scores, -1.0), axis=0, keepdims=True
        )


def unpack_kernel(got_ref, slot_ref, near_ref, align_ref):
    slot = slot_ref[...]
    rank = slot // DEVS
    target = slot - rank * DEVS
    z = target // NQ
    q = target - z * NQ
    from_z = (iota((NZ, ROWS), 0) == z).astype(F32)
    column_of = lax.dot_general(
        got_ref[...], from_z, TN, precision=lax.Precision.HIGHEST, preferred_element_type=F32
    )
    sub = iota((128, ROWS), 0)
    near_ref[...] = jnp.sum(jnp.where(sub == rank * NQ + q, column_of, 0.0), axis=0, keepdims=True)
    align_ref[...] = jnp.sum(jnp.where(sub == (rank + 2) * NQ + q, column_of, 0.0), axis=0, keepdims=True)


def full_exchange(embeddings, ids_row, orders_row, owner_row):
    sds = jax.ShapeDtypeStruct
    packed, _ = call(
        pack_kernel,
        [sds((2 * DEVS, W), BF), sds((1, ROWS), jnp.int32)],
        embeddings,
        ids_row,
        orders_row,
        owner_row,
        scratch=[
            pltpu.VMEM((ROWS, D), F32),
            pltpu.VMEM((1, ROWS), jnp.int32),
            pltpu.VMEM((1, ROWS), jnp.int32),
            pltpu.VMEM((1, DEVS), jnp.int32),
        ],
        far=4,
    )
    send = packed.reshape(2, DEVS, W).transpose(1, 0, 2)
    got = lax.all_to_all(send, ALL, split_axis=0, concat_axis=0, tiled=True)
    rows = got.transpose(1, 0, 2).reshape(2 * DEVS, W)
    center, back = call(owner_kernel, [sds((1, D), F32), sds((4, DEVS), F32)], rows)
    return center, back.reshape(2, 2, NZ, NQ).transpose(0, 3, 1, 2).reshape(2, 2 * DEVS)


def local(embeddings, cluster_ids, orders, owner):
    sds = jax.ShapeDtypeStruct
    ids_row = cluster_ids.reshape(1, ROWS)
    orders_row = orders.reshape(1, ROWS)
    owner_row = owner.reshape(1, DEVS)
    packed, slot = call(
        slab_pack_kernel,
        [sds((SENT, HALF), BF), sds((1, ROWS), jnp.int32)],
        embeddings,
        ids_row,
        orders_row,
        owner_row,
        scratch=[pltpu.VMEM((ROWS, D), F32), pltpu.SemaphoreType.DMA],
        far=1,
    )
    got = lax.all_to_all(packed.reshape(NZ, CHUNK_Z, HALF), "z", split_axis=0, concat_axis=0, tiled=True)
    (moved,) = call(repack_kernel, [sds((NQ, CHUNK, 128), BF)], got)
    rows = lax.all_to_all(moved, SLAB, split_axis=0, concat_axis=0, tiled=True)
    center, back, flag = call(
        slab_owner_kernel,
        [sds((1, D), F32), sds((2, 2 * DEVS), F32), sds((1, 128), F32)],
        rows,
        scratch=[pltpu.VMEM((2 * DEVS, D), BF)],
    )
    flag, *arguments = lax.optimization_barrier((flag, embeddings, ids_row, orders_row, owner_row))
    center, back = lax.cond(
        flag[0, 0] > 0.0,
        lambda: full_exchange(*arguments),
        lambda: (center, back),
    )
    back = back.reshape(2, NQ, NQ).transpose(1, 0, 2).reshape(NQ, 1, 2 * NQ)
    back = lax.all_to_all(back, SLAB, split_axis=0, concat_axis=0, tiled=True)
    back = back.reshape(NQ, 4, NZ).transpose(2, 1, 0).reshape(NZ, 1, 4 * NQ)
    back = lax.all_to_all(back, "z", split_axis=0, concat_axis=0, tiled=True)
    near, align = call(
        unpack_kernel,
        [sds((1, ROWS), F32), sds((1, ROWS), F32)],
        back.reshape(NZ, 4 * NQ),
        slot,
    )
    return (center, near.reshape(ROWS), align.reshape(ROWS))


def solution(mesh):
    fine = Mesh(mesh.devices.reshape(16, 4, 2, 4), ALL)
    return jax.shard_map(
        local,
        mesh=fine,
        in_specs=(P(ALL, None), P(ALL), P(ALL), P()),
        out_specs=(P(ALL, None), P(ALL), P(ALL)),
        check_vma=False,
    )
```

```python
import jax
import jax.numpy as jnp
from jax import lax
from jax.experimental import pallas as pl
from jax.experimental.pallas import tpu as pltpu
from jax.sharding import Mesh
from jax.sharding import PartitionSpec as P

ALL = ("z", "y", "core", "x")
SLAB = ("y", "core", "x")
NZ = 16
NQ = 32
DEVS = NZ * NQ
ROWS = 256
D = 768
W = D + 128
BF = jnp.bfloat16
F32 = jnp.float32
NT = (((1,), (1,)), ((), ()))
TN = (((0,), (0,)), ((), ()))
FIT = 35
HALF = D // 2
CHUNK_Z = 2 * (FIT + 1)
SENT = NZ * CHUNK_Z
MAIN = NZ * NQ
KEPT = MAIN + NZ * 8
COLS = D // 128
CHUNK = COLS * NQ + 8


def column(row):
    return jnp.transpose(jnp.broadcast_to(row, (128, row.shape[1])))[:, :1]


def call(kernel, shapes, *args, scratch=(), far=0):
    return pl.pallas_call(
        kernel,
        out_shape=shapes,
        scratch_shapes=scratch,
        compiler_params=pltpu.CompilerParams(vmem_limit_bytes=24 * 2**20),
        in_specs=[pl.BlockSpec(memory_space=pltpu.HBM if i < far else pltpu.VMEM) for i in range(len(args))],
        out_specs=[pl.BlockSpec(memory_space=pltpu.VMEM) for _ in shapes],
    )(*args)


def targets(ids_row, owner_row):
    hot = (lax.broadcasted_iota(jnp.int32, (DEVS, ROWS), 0) == ids_row).astype(F32).astype(BF)
    high = owner_row // 16
    low = owner_row - high * 16
    sub = lax.broadcasted_iota(jnp.int32, (8, DEVS), 0)
    digits = jnp.where(sub == 0, high, jnp.where(sub == 1, low, 0)).astype(F32).astype(BF)
    found = jnp.dot(digits, hot, preferred_element_type=F32)
    return found[0:1] * 16.0 + found[1:2]


def rank_among_equal(row):
    col = column(row)
    j = lax.broadcasted_iota(jnp.int32, (ROWS, ROWS), 0)
    i = lax.broadcasted_iota(jnp.int32, (ROWS, ROWS), 1)
    return jnp.sum(jnp.where((col == row) & (j < i), 1.0, 0.0), axis=0, keepdims=True)


def pack_kernel(emb_far, ids_far, ord_far, own_far, out_ref, slot_ref, emb_ref, ids_ref, ord_ref, own_ref):
    pltpu.sync_copy(emb_far, emb_ref)
    pltpu.sync_copy(ids_far, ids_ref)
    pltpu.sync_copy(ord_far, ord_ref)
    pltpu.sync_copy(own_far, own_ref)
    target = targets(ids_ref[...], own_ref[...])
    rank = rank_among_equal(target)
    pos = (rank * DEVS + target).astype(jnp.int32)
    slot_ref[...] = pos
    emb = emb_ref[...]
    squares = jnp.sum(emb * emb, axis=1, keepdims=True) + 1e-06
    units = (emb * lax.rsqrt(squares)).astype(BF)
    scale = jnp.sqrt(squares).astype(BF)
    lane = lax.broadcasted_iota(jnp.int32, (ROWS, 128), 1)
    scale_lanes = jnp.where(lane == 0, scale.astype(F32), 0.0).astype(BF)
    order = ord_ref[...]
    high = order // 256
    low = order - high * 256
    sub = lax.broadcasted_iota(jnp.int32, (128, ROWS), 0)
    order_lanes = jnp.where(sub == 1, high + 1, jnp.where(sub == 2, low, 0)).astype(F32).astype(BF)
    for k in range(2):
        place = (lax.broadcasted_iota(jnp.int32, (DEVS, ROWS), 0) + k * DEVS == pos).astype(F32).astype(BF)
        rows = pl.ds(k * DEVS, DEVS)
        out_ref[rows, :D] = jnp.dot(place, units, preferred_element_type=F32).astype(BF)
        meta = jnp.dot(place, scale_lanes, preferred_element_type=F32)
        meta = meta + lax.dot_general(place, order_lanes, NT, preferred_element_type=F32)
        out_ref[rows, D:] = meta.astype(BF)


def owner_kernel(rows_ref, center_ref, back_ref):
    total = 2 * DEVS
    meta = rows_ref[:, D:].astype(F32)
    meta_t = jnp.transpose(meta)
    order_col = (meta[:, 1:2] - 1.0) * 256.0 + meta[:, 2:3]
    key_col = jnp.where(order_col >= 0.0, order_col, 1e6)
    order_row = (meta_t[1:2] - 1.0) * 256.0 + meta_t[2:3]
    members = jnp.sum(jnp.where(order_row >= 0.0, 1.0, 0.0))
    keys = rows_ref[:, :D]
    scale = jnp.broadcast_to(meta_t[0:1], (8, total)).astype(BF)
    center = jnp.dot(scale, keys, preferred_element_type=F32)[0:1] / members
    center_ref[...] = center
    length = lax.rsqrt(jnp.sum(center * center, axis=1, keepdims=True) + 1e-06)
    direction = jnp.broadcast_to(center * length, (8, D)).astype(BF)
    aligned = lax.dot_general(direction, keys, NT, preferred_element_type=F32)[0:1]
    back_ref[2:3] = aligned[:, :DEVS]
    back_ref[3:4] = aligned[:, DEVS:]
    block = 256
    for b in range(total // block):
        scores = lax.dot_general(
            keys, rows_ref[pl.ds(b * block, block), :D], NT, preferred_element_type=F32
        )
        earlier = key_col < order_row[:, b * block : (b + 1) * block]
        best = jnp.max(jnp.where(earlier, scores, -1.0), axis=0, keepdims=True)
        k, first = divmod(b * block, DEVS)
        back_ref[k : k + 1, first : first + block] = best


def row_of(col):
    return jnp.transpose(jnp.broadcast_to(col, (col.shape[0], 128)))[:1]


def iota(shape, dim):
    return lax.broadcasted_iota(jnp.int32, shape, dim)


def hot(condition):
    return condition.astype(F32).astype(BF)


def dot(a, b):
    return jnp.dot(a, b, preferred_element_type=F32)


def dot_nt(a, b):
    return lax.dot_general(a, b, NT, preferred_element_type=F32)


def slab_pack_kernel(emb_ref, ids_ref, ord_ref, own_ref, out_ref, slot_ref, here_ref, sem):
    parts = [pl.ds(i * 64, 64) for i in range(ROWS // 64)]
    copies = [
        pltpu.make_async_copy(emb_ref.at[part, :], here_ref.at[part, :], sem.at[i])
        for i, part in enumerate(parts)
    ]
    for copy in copies:
        copy.start()
    target = targets(ids_ref[...], own_ref[...])
    rank = rank_among_equal(target).astype(jnp.int32)
    whole = target.astype(jnp.int32)
    slot_ref[...] = rank * DEVS + whole
    z = whole // NQ
    q = whole - z * NQ
    place = rank_among_equal(z.astype(F32)).astype(jnp.int32)
    overflow = jnp.max((place >= FIT).astype(F32), axis=1, keepdims=True)
    left = z * CHUNK_Z + jnp.where(place < NQ, place, place + NQ)
    right = left + jnp.where(place < NQ, NQ, 4)
    left = jnp.where(place < FIT, left, -1)
    right = jnp.where(place < FIT, right, -1)
    even = hot(iota((128, ROWS), 0) == place)
    odd = hot(iota((128, ROWS), 0) == place + 64)
    for copy in copies:
        copy.wait()
    emb = here_ref[...]
    squares = jnp.sum(emb * emb, axis=1, keepdims=True) + 1e-06
    units = (emb * lax.rsqrt(squares)).astype(BF)
    scale = row_of(jnp.sqrt(squares).astype(BF).astype(F32))
    order = ord_ref[...]
    high = order // 256
    low = order - high * 256
    sub = iota((NZ * 4, ROWS), 0)
    value = sub // NZ
    picked = jnp.where(
        value == 0,
        scale,
        jnp.where(value == 1, high, jnp.where(value == 2, low, q * 2 + rank + 1)).astype(F32),
    )
    mine = jnp.where(sub - value * NZ == z, picked, 0.0).astype(BF)
    found = [
        (dot_nt(mine[v * NZ : (v + 1) * NZ], even) + dot_nt(mine[(v + 1) * NZ : (v + 2) * NZ], odd)).astype(BF)
        for v in (0, 2)
    ]
    meta = jnp.concatenate(found + [jnp.broadcast_to(overflow, (NZ, 128)).astype(BF)], axis=1)
    last = hot(iota((SENT, NZ), 0) == iota((SENT, NZ), 1) * CHUNK_Z + 67)
    rows = iota((SENT, ROWS), 0)
    sent = dot(hot(rows == left), units[:, :HALF]) + dot(hot(rows == right), units[:, HALF:])
    out_ref[...] = (sent + dot(last, meta)).astype(BF)


def repack_kernel(rows_ref, out_ref):
    main_left = rows_ref[:, :NQ, :].reshape(MAIN, HALF)
    main_right = rows_ref[:, NQ : 2 * NQ, :].reshape(MAIN, HALF)
    tail = rows_ref[:, 2 * NQ :, :].reshape(NZ * 8, HALF)
    meta = dot(hot(iota((NZ, NZ * 8), 1) == iota((NZ, NZ * 8), 0) * 8 + 3), tail)
    flag = jnp.max(meta[:, 256:384])
    pairs = jnp.concatenate([meta[:, :128], meta[:, 128:256]], axis=0).astype(BF)

    def source(shape):
        k = iota(shape, 1)
        t = k - MAIN
        z = jnp.where(t < 0, k // NQ, t // 8)
        place = jnp.where(t < 0, k - z * NQ, NQ + t - (t // 4) * 4)
        return z, place, t

    sub = iota((128, KEPT), 0)
    _, place, _ = source((128, KEPT))
    z, _, _ = source((NZ * 2, KEPT))
    here = iota((NZ * 2, KEPT), 0)
    here = here - (here // NZ) * NZ == z
    evens = jnp.where(here, dot(pairs, hot(sub == place)), 0.0).reshape(2, NZ, KEPT)
    odds = jnp.where(here, dot(pairs, hot(sub == place + 64)), 0.0).reshape(2, NZ, KEPT)
    scale = jnp.sum(evens[0], axis=0, keepdims=True)
    low = jnp.sum(evens[1], axis=0, keepdims=True)
    high = jnp.sum(odds[0], axis=0, keepdims=True)
    code = jnp.sum(odds[1], axis=0, keepdims=True).astype(jnp.int32) - 1
    z, place, t = source((1, KEPT))
    filled = (code >= 0) & (place < FIT)
    q = code // 2
    slot = (code - q * 2) * NZ + z
    is_left = filled & ((t < 0) | (t - (t // 8) * 8 < 4))
    is_right = filled & ((t < 0) | (t - (t // 8) * 8 >= 4))
    left = jnp.where(is_left, q * NQ + slot, -1)
    right = jnp.where(is_right, q * NQ + slot, -1)
    spread = hot(iota((2 * DEVS, MAIN), 0) == left[:, :MAIN])
    rows = iota((2 * DEVS, NZ * 8), 0)
    halves = (
        (dot(spread, main_left) + dot(hot(rows == left[:, MAIN:]), tail)).astype(BF),
        (dot(spread, main_right) + dot(hot(rows == right[:, MAIN:]), tail)).astype(BF),
    )
    for c in range(COLS):
        half, part = divmod(c, COLS // 2)
        block = halves[half][:, part * 128 : (part + 1) * 128]
        out_ref[:, c * NQ : (c + 1) * NQ, :] = block.reshape(NQ, NQ, 128)
    v = iota((8, KEPT), 0)
    eight = jnp.where(v == 0, scale, jnp.where(v == 1, high, jnp.where(v == 2, low, jnp.where(v == 3, 1.0, 0.0))))
    eight = jnp.broadcast_to(eight[None], (NQ, 8, KEPT)).reshape(NQ * 8, KEPT)
    owner = jnp.where(is_left, q, -1)
    mine = jnp.where(iota((NQ * 8, KEPT), 0) // 8 == owner, eight, 0.0).astype(BF)
    details = dot_nt(mine, hot(iota((128, KEPT), 0) == slot))
    sub = iota((NQ * 8, 128), 0)
    details = details + jnp.where(sub - (sub // 8) * 8 == 4, flag, 0.0)
    out_ref[:, COLS * NQ :, :] = details.astype(BF).reshape(NQ, 8, 128)


def slab_owner_kernel(rows_ref, center_ref, back_ref, flag_ref, keys_ref):
    total = 2 * DEVS
    for c in range(COLS):
        keys_ref[:, c * 128 : (c + 1) * 128] = rows_ref[:, c * NQ : (c + 1) * NQ, :].reshape(total, 128)
    details = rows_ref[:, COLS * NQ :, :].reshape(NQ * 8, 128)
    n = iota((128, total), 1)
    along = dot(details, hot(iota((128, total), 0) == n - (n // NQ) * NQ))
    here = iota((NQ * 8, total), 0) // 8 == iota((NQ * 8, total), 1) // NQ
    values = jnp.sum(jnp.where(here, along, 0.0).reshape(NQ, 8, total), axis=0)
    flag_ref[...] = jnp.broadcast_to(jnp.max(values[4:5], axis=1, keepdims=True), (1, 128))
    order_row = values[1:2] * 256.0 + values[2:3]
    members = jnp.sum(values[3:4], axis=1, keepdims=True)
    key_col = column(jnp.where(values[3:4] > 0.0, order_row, 1e6))
    scale = jnp.broadcast_to(values[0:1], (8, total)).astype(BF)
    center = dot(scale, keys_ref[...])[0:1] / members
    center_ref[...] = center
    length = lax.rsqrt(jnp.sum(center * center, axis=1, keepdims=True) + 1e-06)
    direction = jnp.broadcast_to(center * length, (8, D)).astype(BF)
    back_ref[1:2] = dot_nt(direction, keys_ref[...])[0:1]
    block = 256
    for b in range(total // block):
        some = slice(b * block, (b + 1) * block)
        scores = dot_nt(keys_ref[...], keys_ref[some, :])
        back_ref[0:1, some] = jnp.max(
            jnp.where(key_col < order_row[:, some], scores, -1.0), axis=0, keepdims=True
        )


def unpack_kernel(got_ref, slot_ref, near_ref, align_ref):
    slot = slot_ref[...]
    rank = slot // DEVS
    target = slot - rank * DEVS
    z = target // NQ
    q = target - z * NQ
    from_z = (iota((NZ, ROWS), 0) == z).astype(F32)
    column_of = lax.dot_general(
        got_ref[...], from_z, TN, precision=lax.Precision.HIGHEST, preferred_element_type=F32
    )
    sub = iota((128, ROWS), 0)
    near_ref[...] = jnp.sum(jnp.where(sub == rank * NQ + q, column_of, 0.0), axis=0, keepdims=True)
    align_ref[...] = jnp.sum(jnp.where(sub == (rank + 2) * NQ + q, column_of, 0.0), axis=0, keepdims=True)


def full_exchange(embeddings, ids_row, orders_row, owner_row):
    sds = jax.ShapeDtypeStruct
    packed, _ = call(
        pack_kernel,
        [sds((2 * DEVS, W), BF), sds((1, ROWS), jnp.int32)],
        embeddings,
        ids_row,
        orders_row,
        owner_row,
        scratch=[
            pltpu.VMEM((ROWS, D), F32),
            pltpu.VMEM((1, ROWS), jnp.int32),
            pltpu.VMEM((1, ROWS), jnp.int32),
            pltpu.VMEM((1, DEVS), jnp.int32),
        ],
        far=4,
    )
    send = packed.reshape(2, DEVS, W).transpose(1, 0, 2)
    got = lax.all_to_all(send, ALL, split_axis=0, concat_axis=0, tiled=True)
    rows = got.transpose(1, 0, 2).reshape(2 * DEVS, W)
    center, back = call(owner_kernel, [sds((1, D), F32), sds((4, DEVS), F32)], rows)
    return center, back.reshape(2, 2, NZ, NQ).transpose(0, 3, 1, 2).reshape(2, 2 * DEVS)


def local(embeddings, cluster_ids, orders, owner):
    sds = jax.ShapeDtypeStruct
    ids_row = cluster_ids.reshape(1, ROWS)
    orders_row = orders.reshape(1, ROWS)
    owner_row = owner.reshape(1, DEVS)
    packed, slot = call(
        slab_pack_kernel,
        [sds((SENT, HALF), BF), sds((1, ROWS), jnp.int32)],
        embeddings,
        ids_row,
        orders_row,
        owner_row,
        scratch=[pltpu.VMEM((ROWS, D), F32), pltpu.SemaphoreType.DMA((ROWS // 64,))],
        far=1,
    )
    got = lax.all_to_all(packed.reshape(NZ, CHUNK_Z, HALF), "z", split_axis=0, concat_axis=0, tiled=True)
    (moved,) = call(repack_kernel, [sds((NQ, CHUNK, 128), BF)], got)
    rows = lax.all_to_all(moved, SLAB, split_axis=0, concat_axis=0, tiled=True)
    center, back, flag = call(
        slab_owner_kernel,
        [sds((1, D), F32), sds((2, 2 * DEVS), F32), sds((1, 128), F32)],
        rows,
        scratch=[pltpu.VMEM((2 * DEVS, D), BF)],
    )
    flag, *arguments = lax.optimization_barrier((flag, embeddings, ids_row, orders_row, owner_row))
    center, back = lax.cond(
        flag[0, 0] > 0.0,
        lambda: full_exchange(*arguments),
        lambda: (center, back),
    )
    back = back.reshape(2, NQ, NQ).transpose(1, 0, 2).reshape(NQ, 1, 2 * NQ)
    back = lax.all_to_all(back, SLAB, split_axis=0, concat_axis=0, tiled=True)
    back = back.reshape(NQ, 4, NZ).transpose(2, 1, 0).reshape(NZ, 1, 4 * NQ)
    back = lax.all_to_all(back, "z", split_axis=0, concat_axis=0, tiled=True)
    near, align = call(
        unpack_kernel,
        [sds((1, ROWS), F32), sds((1, ROWS), F32)],
        back.reshape(NZ, 4 * NQ),
        slot,
    )
    return (center, near.reshape(ROWS), align.reshape(ROWS))


def solution(mesh):
    fine = Mesh(mesh.devices.reshape(16, 4, 2, 4), ALL)
    return jax.shard_map(
        local,
        mesh=fine,
        in_specs=(P(ALL, None), P(ALL), P(ALL), P()),
        out_specs=(P(ALL, None), P(ALL), P(ALL)),
        check_vma=False,
    )
```

```python
import jax
import jax.numpy as jnp
from jax import lax
from jax.experimental import pallas as pl
from jax.experimental.pallas import tpu as pltpu
from jax.sharding import Mesh
from jax.sharding import PartitionSpec as P

ALL = ("z", "y", "core", "x")
SLAB = ("y", "core", "x")
NZ = 16
NQ = 32
DEVS = NZ * NQ
ROWS = 256
D = 768
W = D + 128
BF = jnp.bfloat16
F32 = jnp.float32
NT = (((1,), (1,)), ((), ()))
TN = (((0,), (0,)), ((), ()))
FIT = 35
HALF = D // 2
CHUNK_Z = 2 * (FIT + 1)
SENT = NZ * CHUNK_Z
MAIN = NZ * NQ
KEPT = MAIN + NZ * 8
COLS = D // 128
CHUNK = COLS * NQ + 8


def column(row):
    return jnp.transpose(jnp.broadcast_to(row, (128, row.shape[1])))[:, :1]


def call(kernel, shapes, *args, scratch=(), far=0):
    return pl.pallas_call(
        kernel,
        out_shape=shapes,
        scratch_shapes=scratch,
        compiler_params=pltpu.CompilerParams(vmem_limit_bytes=24 * 2**20),
        in_specs=[pl.BlockSpec(memory_space=pltpu.HBM if i < far else pltpu.VMEM) for i in range(len(args))],
        out_specs=[pl.BlockSpec(memory_space=pltpu.VMEM) for _ in shapes],
    )(*args)


def targets(ids_row, owner_row):
    hot = (lax.broadcasted_iota(jnp.int32, (DEVS, ROWS), 0) == ids_row).astype(F32).astype(BF)
    high = owner_row // 16
    low = owner_row - high * 16
    sub = lax.broadcasted_iota(jnp.int32, (8, DEVS), 0)
    digits = jnp.where(sub == 0, high, jnp.where(sub == 1, low, 0)).astype(F32).astype(BF)
    found = jnp.dot(digits, hot, preferred_element_type=F32)
    return found[0:1] * 16.0 + found[1:2]


def rank_among_equal(row):
    col = column(row)
    j = lax.broadcasted_iota(jnp.int32, (ROWS, ROWS), 0)
    i = lax.broadcasted_iota(jnp.int32, (ROWS, ROWS), 1)
    return jnp.sum(jnp.where((col == row) & (j < i), 1.0, 0.0), axis=0, keepdims=True)


def pack_kernel(emb_far, ids_far, ord_far, own_far, out_ref, slot_ref, emb_ref, ids_ref, ord_ref, own_ref):
    pltpu.sync_copy(emb_far, emb_ref)
    pltpu.sync_copy(ids_far, ids_ref)
    pltpu.sync_copy(ord_far, ord_ref)
    pltpu.sync_copy(own_far, own_ref)
    target = targets(ids_ref[...], own_ref[...])
    rank = rank_among_equal(target)
    pos = (rank * DEVS + target).astype(jnp.int32)
    slot_ref[...] = pos
    emb = emb_ref[...]
    squares = jnp.sum(emb * emb, axis=1, keepdims=True) + 1e-06
    units = (emb * lax.rsqrt(squares)).astype(BF)
    scale = jnp.sqrt(squares).astype(BF)
    lane = lax.broadcasted_iota(jnp.int32, (ROWS, 128), 1)
    scale_lanes = jnp.where(lane == 0, scale.astype(F32), 0.0).astype(BF)
    order = ord_ref[...]
    high = order // 256
    low = order - high * 256
    sub = lax.broadcasted_iota(jnp.int32, (128, ROWS), 0)
    order_lanes = jnp.where(sub == 1, high + 1, jnp.where(sub == 2, low, 0)).astype(F32).astype(BF)
    for k in range(2):
        place = (lax.broadcasted_iota(jnp.int32, (DEVS, ROWS), 0) + k * DEVS == pos).astype(F32).astype(BF)
        rows = pl.ds(k * DEVS, DEVS)
        out_ref[rows, :D] = jnp.dot(place, units, preferred_element_type=F32).astype(BF)
        meta = jnp.dot(place, scale_lanes, preferred_element_type=F32)
        meta = meta + lax.dot_general(place, order_lanes, NT, preferred_element_type=F32)
        out_ref[rows, D:] = meta.astype(BF)


def owner_kernel(rows_ref, center_ref, back_ref):
    total = 2 * DEVS
    meta = rows_ref[:, D:].astype(F32)
    meta_t = jnp.transpose(meta)
    order_col = (meta[:, 1:2] - 1.0) * 256.0 + meta[:, 2:3]
    key_col = jnp.where(order_col >= 0.0, order_col, 1e6)
    order_row = (meta_t[1:2] - 1.0) * 256.0 + meta_t[2:3]
    members = jnp.sum(jnp.where(order_row >= 0.0, 1.0, 0.0))
    keys = rows_ref[:, :D]
    scale = jnp.broadcast_to(meta_t[0:1], (8, total)).astype(BF)
    center = jnp.dot(scale, keys, preferred_element_type=F32)[0:1] / members
    center_ref[...] = center
    length = lax.rsqrt(jnp.sum(center * center, axis=1, keepdims=True) + 1e-06)
    direction = jnp.broadcast_to(center * length, (8, D)).astype(BF)
    aligned = lax.dot_general(direction, keys, NT, preferred_element_type=F32)[0:1]
    back_ref[2:3] = aligned[:, :DEVS]
    back_ref[3:4] = aligned[:, DEVS:]
    block = 256
    for b in range(total // block):
        scores = lax.dot_general(
            keys, rows_ref[pl.ds(b * block, block), :D], NT, preferred_element_type=F32
        )
        earlier = key_col < order_row[:, b * block : (b + 1) * block]
        best = jnp.max(jnp.where(earlier, scores, -1.0), axis=0, keepdims=True)
        k, first = divmod(b * block, DEVS)
        back_ref[k : k + 1, first : first + block] = best


def row_of(col):
    return jnp.transpose(jnp.broadcast_to(col, (col.shape[0], 128)))[:1]


def iota(shape, dim):
    return lax.broadcasted_iota(jnp.int32, shape, dim)


def hot(condition):
    return condition.astype(F32).astype(BF)


def dot(a, b):
    return jnp.dot(a, b, preferred_element_type=F32)


def dot_nt(a, b):
    return lax.dot_general(a, b, NT, preferred_element_type=F32)


def slab_pack_kernel(emb_ref, ids_ref, ord_ref, own_ref, out_ref, slot_ref):
    target = targets(ids_ref[...], own_ref[...])
    rank = rank_among_equal(target).astype(jnp.int32)
    whole = target.astype(jnp.int32)
    slot_ref[...] = rank * DEVS + whole
    z = whole // NQ
    q = whole - z * NQ
    place = rank_among_equal(z.astype(F32)).astype(jnp.int32)
    overflow = jnp.max((place >= FIT).astype(F32), axis=1, keepdims=True)
    left = z * CHUNK_Z + jnp.where(place < NQ, place, place + NQ)
    right = left + jnp.where(place < NQ, NQ, 4)
    left = jnp.where(place < FIT, left, -1)
    right = jnp.where(place < FIT, right, -1)
    emb = emb_ref[...]
    squares = jnp.sum(emb * emb, axis=1, keepdims=True) + 1e-06
    units = (emb * lax.rsqrt(squares)).astype(BF)
    scale = row_of(jnp.sqrt(squares).astype(BF).astype(F32))
    order = ord_ref[...]
    high = order // 256
    low = order - high * 256
    sub = iota((NZ * 4, ROWS), 0)
    value = sub // NZ
    picked = jnp.where(
        value == 0,
        scale,
        jnp.where(value == 1, high, jnp.where(value == 2, low, q * 2 + rank + 1)).astype(F32),
    )
    mine = jnp.where(sub - value * NZ == z, picked, 0.0).astype(BF)
    even = hot(iota((128, ROWS), 0) == place)
    odd = hot(iota((128, ROWS), 0) == place + 64)
    found = [
        (dot_nt(mine[v * NZ : (v + 1) * NZ], even) + dot_nt(mine[(v + 1) * NZ : (v + 2) * NZ], odd)).astype(BF)
        for v in (0, 2)
    ]
    meta = jnp.concatenate(found + [jnp.broadcast_to(overflow, (NZ, 128)).astype(BF)], axis=1)
    rows = iota((SENT, ROWS), 0)
    last = hot(iota((SENT, NZ), 0) == iota((SENT, NZ), 1) * CHUNK_Z + 67)
    sent = dot(hot(rows == left), units[:, :HALF]) + dot(hot(rows == right), units[:, HALF:])
    out_ref[...] = (sent + dot(last, meta)).astype(BF)


def repack_kernel(rows_ref, out_ref):
    main_left = rows_ref[:, :NQ, :].reshape(MAIN, HALF)
    main_right = rows_ref[:, NQ : 2 * NQ, :].reshape(MAIN, HALF)
    tail = rows_ref[:, 2 * NQ :, :].reshape(NZ * 8, HALF)
    meta = dot(hot(iota((NZ, NZ * 8), 1) == iota((NZ, NZ * 8), 0) * 8 + 3), tail)
    flag = jnp.max(meta[:, 256:384])
    pairs = jnp.concatenate([meta[:, :128], meta[:, 128:256]], axis=0).astype(BF)

    def source(shape):
        k = iota(shape, 1)
        t = k - MAIN
        z = jnp.where(t < 0, k // NQ, t // 8)
        place = jnp.where(t < 0, k - z * NQ, NQ + t - (t // 4) * 4)
        return z, place, t

    sub = iota((128, KEPT), 0)
    _, place, _ = source((128, KEPT))
    z, _, _ = source((NZ * 2, KEPT))
    here = iota((NZ * 2, KEPT), 0)
    here = here - (here // NZ) * NZ == z
    evens = jnp.where(here, dot(pairs, hot(sub == place)), 0.0).reshape(2, NZ, KEPT)
    odds = jnp.where(here, dot(pairs, hot(sub == place + 64)), 0.0).reshape(2, NZ, KEPT)
    scale = jnp.sum(evens[0], axis=0, keepdims=True)
    low = jnp.sum(evens[1], axis=0, keepdims=True)
    high = jnp.sum(odds[0], axis=0, keepdims=True)
    code = jnp.sum(odds[1], axis=0, keepdims=True).astype(jnp.int32) - 1
    z, place, t = source((1, KEPT))
    filled = (code >= 0) & (place < FIT)
    q = code // 2
    slot = (code - q * 2) * NZ + z
    is_left = filled & ((t < 0) | (t - (t // 8) * 8 < 4))
    is_right = filled & ((t < 0) | (t - (t // 8) * 8 >= 4))
    left = jnp.where(is_left, q * NQ + slot, -1)
    right = jnp.where(is_right, q * NQ + slot, -1)
    spread = hot(iota((2 * DEVS, MAIN), 0) == left[:, :MAIN])
    rows = iota((2 * DEVS, NZ * 8), 0)
    halves = (
        (dot(spread, main_left) + dot(hot(rows == left[:, MAIN:]), tail)).astype(BF),
        (dot(spread, main_right) + dot(hot(rows == right[:, MAIN:]), tail)).astype(BF),
    )
    for c in range(COLS):
        half, part = divmod(c, COLS // 2)
        block = halves[half][:, part * 128 : (part + 1) * 128]
        out_ref[:, c * NQ : (c + 1) * NQ, :] = block.reshape(NQ, NQ, 128)
    v = iota((8, KEPT), 0)
    eight = jnp.where(v == 0, scale, jnp.where(v == 1, high, jnp.where(v == 2, low, jnp.where(v == 3, 1.0, 0.0))))
    eight = jnp.broadcast_to(eight[None], (NQ, 8, KEPT)).reshape(NQ * 8, KEPT)
    owner = jnp.where(is_left, q, -1)
    mine = jnp.where(iota((NQ * 8, KEPT), 0) // 8 == owner, eight, 0.0).astype(BF)
    details = dot_nt(mine, hot(iota((128, KEPT), 0) == slot))
    sub = iota((NQ * 8, 128), 0)
    details = details + jnp.where(sub - (sub // 8) * 8 == 4, flag, 0.0)
    out_ref[:, COLS * NQ :, :] = details.astype(BF).reshape(NQ, 8, 128)


def slab_owner_kernel(rows_ref, center_ref, back_ref, flag_ref, keys_ref):
    total = 2 * DEVS
    for c in range(COLS):
        keys_ref[:, c * 128 : (c + 1) * 128] = rows_ref[:, c * NQ : (c + 1) * NQ, :].reshape(total, 128)
    details = rows_ref[:, COLS * NQ :, :].reshape(NQ * 8, 128)
    n = iota((128, total), 1)
    along = dot(details, hot(iota((128, total), 0) == n - (n // NQ) * NQ))
    here = iota((NQ * 8, total), 0) // 8 == iota((NQ * 8, total), 1) // NQ
    values = jnp.sum(jnp.where(here, along, 0.0).reshape(NQ, 8, total), axis=0)
    flag_ref[...] = jnp.broadcast_to(jnp.max(values[4:5], axis=1, keepdims=True), (1, 128))
    order_row = values[1:2] * 256.0 + values[2:3]
    members = jnp.sum(values[3:4], axis=1, keepdims=True)
    key_col = column(jnp.where(values[3:4] > 0.0, order_row, 1e6))
    scale = jnp.broadcast_to(values[0:1], (8, total)).astype(BF)
    center = dot(scale, keys_ref[...])[0:1] / members
    center_ref[...] = center
    length = lax.rsqrt(jnp.sum(center * center, axis=1, keepdims=True) + 1e-06)
    direction = jnp.broadcast_to(center * length, (8, D)).astype(BF)
    back_ref[1:2] = dot_nt(direction, keys_ref[...])[0:1]
    block = 256
    for b in range(total // block):
        some = slice(b * block, (b + 1) * block)
        scores = dot_nt(keys_ref[...], keys_ref[some, :])
        back_ref[0:1, some] = jnp.max(
            jnp.where(key_col < order_row[:, some], scores, -1.0), axis=0, keepdims=True
        )


def unpack_kernel(got_ref, slot_ref, near_ref, align_ref):
    slot = slot_ref[...]
    rank = slot // DEVS
    target = slot - rank * DEVS
    z = target // NQ
    q = target - z * NQ
    from_z = (iota((NZ, ROWS), 0) == z).astype(F32)
    column_of = lax.dot_general(
        got_ref[...], from_z, TN, precision=lax.Precision.HIGHEST, preferred_element_type=F32
    )
    sub = iota((128, ROWS), 0)
    near_ref[...] = jnp.sum(jnp.where(sub == rank * NQ + q, column_of, 0.0), axis=0, keepdims=True)
    align_ref[...] = jnp.sum(jnp.where(sub == (rank + 2) * NQ + q, column_of, 0.0), axis=0, keepdims=True)


def full_exchange(embeddings, ids_row, orders_row, owner_row):
    sds = jax.ShapeDtypeStruct
    packed, _ = call(
        pack_kernel,
        [sds((2 * DEVS, W), BF), sds((1, ROWS), jnp.int32)],
        embeddings,
        ids_row,
        orders_row,
        owner_row,
        scratch=[
            pltpu.VMEM((ROWS, D), F32),
            pltpu.VMEM((1, ROWS), jnp.int32),
            pltpu.VMEM((1, ROWS), jnp.int32),
            pltpu.VMEM((1, DEVS), jnp.int32),
        ],
        far=4,
    )
    send = packed.reshape(2, DEVS, W).transpose(1, 0, 2)
    got = lax.all_to_all(send, ALL, split_axis=0, concat_axis=0, tiled=True)
    rows = got.transpose(1, 0, 2).reshape(2 * DEVS, W)
    center, back = call(owner_kernel, [sds((1, D), F32), sds((4, DEVS), F32)], rows)
    return center, back.reshape(2, 2, NZ, NQ).transpose(0, 3, 1, 2).reshape(2, 2 * DEVS)


def local(embeddings, cluster_ids, orders, owner):
    sds = jax.ShapeDtypeStruct
    ids_row = cluster_ids.reshape(1, ROWS)
    orders_row = orders.reshape(1, ROWS)
    owner_row = owner.reshape(1, DEVS)
    packed, slot = call(
        slab_pack_kernel,
        [sds((SENT, HALF), BF), sds((1, ROWS), jnp.int32)],
        embeddings,
        ids_row,
        orders_row,
        owner_row,
    )
    got = lax.all_to_all(packed.reshape(NZ, CHUNK_Z, HALF), "z", split_axis=0, concat_axis=0, tiled=True)
    (moved,) = call(repack_kernel, [sds((NQ, CHUNK, 128), BF)], got)
    rows = lax.all_to_all(moved, SLAB, split_axis=0, concat_axis=0, tiled=True)
    center, back, flag = call(
        slab_owner_kernel,
        [sds((1, D), F32), sds((2, 2 * DEVS), F32), sds((1, 128), F32)],
        rows,
        scratch=[pltpu.VMEM((2 * DEVS, D), BF)],
    )
    flag, *arguments = lax.optimization_barrier((flag, embeddings, ids_row, orders_row, owner_row))
    center, back = lax.cond(
        flag[0, 0] > 0.0,
        lambda: full_exchange(*arguments),
        lambda: (center, back),
    )
    back = back.reshape(2, NQ, NQ).transpose(1, 0, 2).reshape(NQ, 1, 2 * NQ)
    back = lax.all_to_all(back, SLAB, split_axis=0, concat_axis=0, tiled=True)
    back = back.reshape(NQ, 4, NZ).transpose(2, 1, 0).reshape(NZ, 1, 4 * NQ)
    back = lax.all_to_all(back, "z", split_axis=0, concat_axis=0, tiled=True)
    near, align = call(
        unpack_kernel,
        [sds((1, ROWS), F32), sds((1, ROWS), F32)],
        back.reshape(NZ, 4 * NQ),
        slot,
    )
    return (center, near.reshape(ROWS), align.reshape(ROWS))


def solution(mesh):
    fine = Mesh(mesh.devices.reshape(16, 4, 2, 4), ALL)
    return jax.shard_map(
        local,
        mesh=fine,
        in_specs=(P(ALL, None), P(ALL), P(ALL), P()),
        out_specs=(P(ALL, None), P(ALL), P(ALL)),
        check_vma=False,
    )
```

```python
import jax
import jax.numpy as jnp
from jax import lax
from jax.experimental import pallas as pl
from jax.experimental.pallas import tpu as pltpu
from jax.sharding import Mesh
from jax.sharding import PartitionSpec as P

ALL = ("z", "y", "core", "x")
SLAB = ("y", "core", "x")
NZ = 16
NQ = 32
DEVS = NZ * NQ
ROWS = 256
D = 768
W = D + 128
BF = jnp.bfloat16
F32 = jnp.float32
NT = (((1,), (1,)), ((), ()))
TN = (((0,), (0,)), ((), ()))
FIT = 35
HALF = D // 2
CHUNK_Z = 2 * (FIT + 1)
SENT = NZ * CHUNK_Z
MAIN = NZ * NQ
KEPT = MAIN + NZ * 8
COLS = D // 128
CHUNK = COLS * NQ + 8


def column(row):
    return jnp.transpose(jnp.broadcast_to(row, (128, row.shape[1])))[:, :1]


def call(kernel, shapes, *args, scratch=(), far=0):
    return pl.pallas_call(
        kernel,
        out_shape=shapes,
        scratch_shapes=scratch,
        compiler_params=pltpu.CompilerParams(vmem_limit_bytes=24 * 2**20),
        in_specs=[pl.BlockSpec(memory_space=pltpu.HBM if i < far else pltpu.VMEM) for i in range(len(args))],
        out_specs=[pl.BlockSpec(memory_space=pltpu.VMEM) for _ in shapes],
    )(*args)


def targets(ids_row, owner_row):
    hot = (lax.broadcasted_iota(jnp.int32, (DEVS, ROWS), 0) == ids_row).astype(F32).astype(BF)
    high = owner_row // 16
    low = owner_row - high * 16
    sub = lax.broadcasted_iota(jnp.int32, (8, DEVS), 0)
    digits = jnp.where(sub == 0, high, jnp.where(sub == 1, low, 0)).astype(F32).astype(BF)
    found = jnp.dot(digits, hot, preferred_element_type=F32)
    return found[0:1] * 16.0 + found[1:2]


def rank_among_equal(row):
    col = column(row)
    j = lax.broadcasted_iota(jnp.int32, (ROWS, ROWS), 0)
    i = lax.broadcasted_iota(jnp.int32, (ROWS, ROWS), 1)
    return jnp.sum(jnp.where((col == row) & (j < i), 1.0, 0.0), axis=0, keepdims=True)


def pack_kernel(emb_far, ids_far, ord_far, own_far, out_ref, slot_ref, emb_ref, ids_ref, ord_ref, own_ref):
    pltpu.sync_copy(emb_far, emb_ref)
    pltpu.sync_copy(ids_far, ids_ref)
    pltpu.sync_copy(ord_far, ord_ref)
    pltpu.sync_copy(own_far, own_ref)
    target = targets(ids_ref[...], own_ref[...])
    rank = rank_among_equal(target)
    pos = (rank * DEVS + target).astype(jnp.int32)
    slot_ref[...] = pos
    emb = emb_ref[...]
    squares = jnp.sum(emb * emb, axis=1, keepdims=True) + 1e-06
    units = (emb * lax.rsqrt(squares)).astype(BF)
    scale = jnp.sqrt(squares).astype(BF)
    lane = lax.broadcasted_iota(jnp.int32, (ROWS, 128), 1)
    scale_lanes = jnp.where(lane == 0, scale.astype(F32), 0.0).astype(BF)
    order = ord_ref[...]
    high = order // 256
    low = order - high * 256
    sub = lax.broadcasted_iota(jnp.int32, (128, ROWS), 0)
    order_lanes = jnp.where(sub == 1, high + 1, jnp.where(sub == 2, low, 0)).astype(F32).astype(BF)
    for k in range(2):
        place = (lax.broadcasted_iota(jnp.int32, (DEVS, ROWS), 0) + k * DEVS == pos).astype(F32).astype(BF)
        rows = pl.ds(k * DEVS, DEVS)
        out_ref[rows, :D] = jnp.dot(place, units, preferred_element_type=F32).astype(BF)
        meta = jnp.dot(place, scale_lanes, preferred_element_type=F32)
        meta = meta + lax.dot_general(place, order_lanes, NT, preferred_element_type=F32)
        out_ref[rows, D:] = meta.astype(BF)


def owner_kernel(rows_ref, center_ref, back_ref):
    total = 2 * DEVS
    meta = rows_ref[:, D:].astype(F32)
    meta_t = jnp.transpose(meta)
    order_col = (meta[:, 1:2] - 1.0) * 256.0 + meta[:, 2:3]
    key_col = jnp.where(order_col >= 0.0, order_col, 1e6)
    order_row = (meta_t[1:2] - 1.0) * 256.0 + meta_t[2:3]
    members = jnp.sum(jnp.where(order_row >= 0.0, 1.0, 0.0))
    keys = rows_ref[:, :D]
    scale = jnp.broadcast_to(meta_t[0:1], (8, total)).astype(BF)
    center = jnp.dot(scale, keys, preferred_element_type=F32)[0:1] / members
    center_ref[...] = center
    length = lax.rsqrt(jnp.sum(center * center, axis=1, keepdims=True) + 1e-06)
    direction = jnp.broadcast_to(center * length, (8, D)).astype(BF)
    aligned = lax.dot_general(direction, keys, NT, preferred_element_type=F32)[0:1]
    back_ref[2:3] = aligned[:, :DEVS]
    back_ref[3:4] = aligned[:, DEVS:]
    block = 256
    for b in range(total // block):
        scores = lax.dot_general(
            keys, rows_ref[pl.ds(b * block, block), :D], NT, preferred_element_type=F32
        )
        earlier = key_col < order_row[:, b * block : (b + 1) * block]
        best = jnp.max(jnp.where(earlier, scores, -1.0), axis=0, keepdims=True)
        k, first = divmod(b * block, DEVS)
        back_ref[k : k + 1, first : first + block] = best


def row_of(col):
    return jnp.transpose(jnp.broadcast_to(col, (col.shape[0], 128)))[:1]


def iota(shape, dim):
    return lax.broadcasted_iota(jnp.int32, shape, dim)


def hot(condition):
    return condition.astype(F32).astype(BF)


def dot(a, b):
    return jnp.dot(a, b, preferred_element_type=F32)


def dot_nt(a, b):
    return lax.dot_general(a, b, NT, preferred_element_type=F32)


def slab_pack_kernel(emb_ref, ids_ref, ord_ref, own_ref, out_ref, slot_ref):
    target = targets(ids_ref[...], own_ref[...])
    rank = rank_among_equal(target).astype(jnp.int32)
    whole = target.astype(jnp.int32)
    slot_ref[...] = rank * DEVS + whole
    z = whole // NQ
    q = whole - z * NQ
    place = rank_among_equal(z.astype(F32)).astype(jnp.int32)
    overflow = jnp.max((place >= FIT).astype(F32), axis=1, keepdims=True)
    left = z * CHUNK_Z + jnp.where(place < NQ, place, place + NQ)
    right = left + jnp.where(place < NQ, NQ, 4)
    left = jnp.where(place < FIT, left, -1)
    right = jnp.where(place < FIT, right, -1)
    emb = emb_ref[...]
    squares = jnp.sum(emb * emb, axis=1, keepdims=True) + 1e-06
    units = (emb * lax.rsqrt(squares)).astype(BF)
    scale = row_of(jnp.sqrt(squares).astype(BF).astype(F32))
    order = ord_ref[...]
    high = order // 256
    low = order - high * 256
    sub = iota((NZ * 4, ROWS), 0)
    value = sub // NZ
    picked = jnp.where(
        value == 0,
        scale,
        jnp.where(value == 1, high, jnp.where(value == 2, low, q * 2 + rank + 1)).astype(F32),
    )
    mine = jnp.where(sub - value * NZ == z, picked, 0.0).astype(BF)
    even = hot(iota((128, ROWS), 0) == place)
    odd = hot(iota((128, ROWS), 0) == place + 64)
    found = [
        (dot_nt(mine[v * NZ : (v + 1) * NZ], even) + dot_nt(mine[(v + 1) * NZ : (v + 2) * NZ], odd)).astype(BF)
        for v in (0, 2)
    ]
    meta = jnp.concatenate(found + [jnp.broadcast_to(overflow, (NZ, 128)).astype(BF)], axis=1)
    rows = iota((SENT, ROWS), 0)
    last = hot(iota((SENT, NZ), 0) == iota((SENT, NZ), 1) * CHUNK_Z + 67)
    sent = dot(hot(rows == left), units[:, :HALF]) + dot(hot(rows == right), units[:, HALF:])
    out_ref[...] = (sent + dot(last, meta)).astype(BF)


def repack_kernel(rows_ref, out_ref):
    main_left = rows_ref[:, :NQ, :].reshape(MAIN, HALF)
    main_right = rows_ref[:, NQ : 2 * NQ, :].reshape(MAIN, HALF)
    tail = rows_ref[:, 2 * NQ :, :].reshape(NZ * 8, HALF)
    meta = dot(hot(iota((NZ, NZ * 8), 1) == iota((NZ, NZ * 8), 0) * 8 + 3), tail)
    flag = jnp.max(meta[:, 256:384])
    pairs = jnp.concatenate([meta[:, :128], meta[:, 128:256]], axis=0).astype(BF)

    def source(shape):
        k = iota(shape, 1)
        t = k - MAIN
        z = jnp.where(t < 0, k // NQ, t // 8)
        place = jnp.where(t < 0, k - z * NQ, NQ + t - (t // 4) * 4)
        return z, place, t

    sub = iota((128, KEPT), 0)
    _, place, _ = source((128, KEPT))
    z, _, _ = source((NZ * 2, KEPT))
    here = iota((NZ * 2, KEPT), 0)
    here = here - (here // NZ) * NZ == z
    evens = jnp.where(here, dot(pairs, hot(sub == place)), 0.0).reshape(2, NZ, KEPT)
    odds = jnp.where(here, dot(pairs, hot(sub == place + 64)), 0.0).reshape(2, NZ, KEPT)
    scale = jnp.sum(evens[0], axis=0, keepdims=True)
    low = jnp.sum(evens[1], axis=0, keepdims=True)
    high = jnp.sum(odds[0], axis=0, keepdims=True)
    code = jnp.sum(odds[1], axis=0, keepdims=True).astype(jnp.int32) - 1
    z, place, t = source((1, KEPT))
    filled = (code >= 0) & (place < FIT)
    q = code // 2
    slot = (code - q * 2) * NZ + z
    is_left = filled & ((t < 0) | (t - (t // 8) * 8 < 4))
    is_right = filled & ((t < 0) | (t - (t // 8) * 8 >= 4))
    left = jnp.where(is_left, q * NQ + slot, -1)
    right = jnp.where(is_right, q * NQ + slot, -1)
    spread = hot(iota((2 * DEVS, MAIN), 0) == left[:, :MAIN])
    rows = iota((2 * DEVS, NZ * 8), 0)
    halves = (
        (dot(spread, main_left) + dot(hot(rows == left[:, MAIN:]), tail)).astype(BF),
        (dot(spread, main_right) + dot(hot(rows == right[:, MAIN:]), tail)).astype(BF),
    )
    for c in range(COLS):
        half, part = divmod(c, COLS // 2)
        block = halves[half][:, part * 128 : (part + 1) * 128]
        out_ref[:, c * NQ : (c + 1) * NQ, :] = block.reshape(NQ, NQ, 128)
    v = iota((8, KEPT), 0)
    eight = jnp.where(v == 0, scale, jnp.where(v == 1, high, jnp.where(v == 2, low, jnp.where(v == 3, 1.0, 0.0))))
    eight = jnp.broadcast_to(eight[None], (NQ, 8, KEPT)).reshape(NQ * 8, KEPT)
    owner = jnp.where(is_left, q, -1)
    mine = jnp.where(iota((NQ * 8, KEPT), 0) // 8 == owner, eight, 0.0).astype(BF)
    details = dot_nt(mine, hot(iota((128, KEPT), 0) == slot))
    sub = iota((NQ * 8, 128), 0)
    details = details + jnp.where(sub - (sub // 8) * 8 == 4, flag, 0.0)
    out_ref[:, COLS * NQ :, :] = details.astype(BF).reshape(NQ, 8, 128)


def slab_owner_kernel(rows_ref, center_ref, back_ref, flag_ref, keys_ref):
    total = 2 * DEVS
    for c in range(COLS):
        keys_ref[:, c * 128 : (c + 1) * 128] = rows_ref[:, c * NQ : (c + 1) * NQ, :].reshape(total, 128)
    details = rows_ref[:, COLS * NQ :, :].reshape(NQ * 8, 128)
    n = iota((128, total), 1)
    along = dot(details, hot(iota((128, total), 0) == n - (n // NQ) * NQ))
    here = iota((NQ * 8, total), 0) // 8 == iota((NQ * 8, total), 1) // NQ
    values = jnp.sum(jnp.where(here, along, 0.0).reshape(NQ, 8, total), axis=0)
    flag_ref[...] = jnp.broadcast_to(jnp.max(values[4:5], axis=1, keepdims=True), (1, 128))
    order_row = values[1:2] * 256.0 + values[2:3]
    members = jnp.sum(values[3:4], axis=1, keepdims=True)
    key_col = column(jnp.where(values[3:4] > 0.0, order_row, 1e6))
    scale = jnp.broadcast_to(values[0:1], (8, total)).astype(BF)
    center = dot(scale, keys_ref[...])[0:1] / members
    center_ref[...] = center
    length = lax.rsqrt(jnp.sum(center * center, axis=1, keepdims=True) + 1e-06)
    direction = jnp.broadcast_to(center * length, (8, D)).astype(BF)
    back_ref[1:2] = dot_nt(direction, keys_ref[...])[0:1]
    key_row = jnp.where(values[3:4] > 0.0, order_row, 1e6)
    block = 256
    best = []
    across = []
    for b in range(total // block):
        mine = slice(b * block, (b + 1) * block)
        row = None
        for a in range(b + 1):
            other = slice(a * block, (a + 1) * block)
            scores = dot_nt(keys_ref[other, :], keys_ref[mine, :])
            found = jnp.where(key_col[other] < order_row[:, mine], scores, -1.0)
            found = jnp.max(found, axis=0, keepdims=True)
            row = found if row is None else jnp.maximum(row, found)
            if a < b:
                found = jnp.where(key_row[:, mine] < key_col[other], scores, -1.0)
                found = jnp.max(found, axis=1, keepdims=True)
                across[a] = found if across[a] is None else jnp.maximum(across[a], found)
        best.append(row)
        across.append(None)
    for b, row in enumerate(best):
        if across[b] is not None:
            row = jnp.maximum(row, row_of(across[b]))
        back_ref[0:1, b * block : (b + 1) * block] = row


def unpack_kernel(got_ref, slot_ref, near_ref, align_ref):
    slot = slot_ref[...]
    rank = slot // DEVS
    target = slot - rank * DEVS
    z = target // NQ
    q = target - z * NQ
    from_z = (iota((NZ, ROWS), 0) == z).astype(F32)
    column_of = lax.dot_general(
        got_ref[...], from_z, TN, precision=lax.Precision.HIGHEST, preferred_element_type=F32
    )
    sub = iota((128, ROWS), 0)
    near_ref[...] = jnp.sum(jnp.where(sub == rank * NQ + q, column_of, 0.0), axis=0, keepdims=True)
    align_ref[...] = jnp.sum(jnp.where(sub == (rank + 2) * NQ + q, column_of, 0.0), axis=0, keepdims=True)


def full_exchange(embeddings, ids_row, orders_row, owner_row):
    sds = jax.ShapeDtypeStruct
    packed, _ = call(
        pack_kernel,
        [sds((2 * DEVS, W), BF), sds((1, ROWS), jnp.int32)],
        embeddings,
        ids_row,
        orders_row,
        owner_row,
        scratch=[
            pltpu.VMEM((ROWS, D), F32),
            pltpu.VMEM((1, ROWS), jnp.int32),
            pltpu.VMEM((1, ROWS), jnp.int32),
            pltpu.VMEM((1, DEVS), jnp.int32),
        ],
        far=4,
    )
    send = packed.reshape(2, DEVS, W).transpose(1, 0, 2)
    got = lax.all_to_all(send, ALL, split_axis=0, concat_axis=0, tiled=True)
    rows = got.transpose(1, 0, 2).reshape(2 * DEVS, W)
    center, back = call(owner_kernel, [sds((1, D), F32), sds((4, DEVS), F32)], rows)
    return center, back.reshape(2, 2, NZ, NQ).transpose(0, 3, 1, 2).reshape(2, 2 * DEVS)


def local(embeddings, cluster_ids, orders, owner):
    sds = jax.ShapeDtypeStruct
    ids_row = cluster_ids.reshape(1, ROWS)
    orders_row = orders.reshape(1, ROWS)
    owner_row = owner.reshape(1, DEVS)
    packed, slot = call(
        slab_pack_kernel,
        [sds((SENT, HALF), BF), sds((1, ROWS), jnp.int32)],
        embeddings,
        ids_row,
        orders_row,
        owner_row,
    )
    got = lax.all_to_all(packed.reshape(NZ, CHUNK_Z, HALF), "z", split_axis=0, concat_axis=0, tiled=True)
    (moved,) = call(repack_kernel, [sds((NQ, CHUNK, 128), BF)], got)
    rows = lax.all_to_all(moved, SLAB, split_axis=0, concat_axis=0, tiled=True)
    center, back, flag = call(
        slab_owner_kernel,
        [sds((1, D), F32), sds((2, 2 * DEVS), F32), sds((1, 128), F32)],
        rows,
        scratch=[pltpu.VMEM((2 * DEVS, D), BF)],
    )
    flag, *arguments = lax.optimization_barrier((flag, embeddings, ids_row, orders_row, owner_row))
    center, back = lax.cond(
        flag[0, 0] > 0.0,
        lambda: full_exchange(*arguments),
        lambda: (center, back),
    )
    back = back.reshape(2, NQ, NQ).transpose(1, 0, 2).reshape(NQ, 1, 2 * NQ)
    back = lax.all_to_all(back, SLAB, split_axis=0, concat_axis=0, tiled=True)
    back = back.reshape(NQ, 4, NZ).transpose(2, 1, 0).reshape(NZ, 1, 4 * NQ)
    back = lax.all_to_all(back, "z", split_axis=0, concat_axis=0, tiled=True)
    near, align = call(
        unpack_kernel,
        [sds((1, ROWS), F32), sds((1, ROWS), F32)],
        back.reshape(NZ, 4 * NQ),
        slot,
    )
    return (center, near.reshape(ROWS), align.reshape(ROWS))


def solution(mesh):
    fine = Mesh(mesh.devices.reshape(16, 4, 2, 4), ALL)
    return jax.shard_map(
        local,
        mesh=fine,
        in_specs=(P(ALL, None), P(ALL), P(ALL), P()),
        out_specs=(P(ALL, None), P(ALL), P(ALL)),
        check_vma=False,
    )
```

```python
import jax
import jax.numpy as jnp
from jax import lax
from jax.experimental import pallas as pl
from jax.experimental.pallas import tpu as pltpu
from jax.sharding import Mesh
from jax.sharding import PartitionSpec as P

ALL = ("z", "y", "core", "x")
SLAB = ("y", "core", "x")
NZ = 16
NQ = 32
DEVS = NZ * NQ
ROWS = 256
D = 768
W = D + 128
BF = jnp.bfloat16
F32 = jnp.float32
NT = (((1,), (1,)), ((), ()))
TN = (((0,), (0,)), ((), ()))
FIT = 35
HALF = D // 2
CHUNK_Z = 2 * (FIT + 1)
SENT = NZ * CHUNK_Z
MAIN = NZ * NQ
KEPT = MAIN + NZ * 8
COLS = D // 128
CHUNK = COLS * NQ + 8


def column(row):
    return jnp.transpose(jnp.broadcast_to(row, (128, row.shape[1])))[:, :1]


def call(kernel, shapes, *args, scratch=(), far=0):
    return pl.pallas_call(
        kernel,
        out_shape=shapes,
        scratch_shapes=scratch,
        compiler_params=pltpu.CompilerParams(vmem_limit_bytes=24 * 2**20),
        in_specs=[pl.BlockSpec(memory_space=pltpu.HBM if i < far else pltpu.VMEM) for i in range(len(args))],
        out_specs=[pl.BlockSpec(memory_space=pltpu.VMEM) for _ in shapes],
    )(*args)


def targets(ids_row, owner_row):
    hot = (lax.broadcasted_iota(jnp.int32, (DEVS, ROWS), 0) == ids_row).astype(F32).astype(BF)
    high = owner_row // 16
    low = owner_row - high * 16
    sub = lax.broadcasted_iota(jnp.int32, (8, DEVS), 0)
    digits = jnp.where(sub == 0, high, jnp.where(sub == 1, low, 0)).astype(F32).astype(BF)
    found = jnp.dot(digits, hot, preferred_element_type=F32)
    return found[0:1] * 16.0 + found[1:2]


def rank_among_equal(row):
    col = column(row)
    j = lax.broadcasted_iota(jnp.int32, (ROWS, ROWS), 0)
    i = lax.broadcasted_iota(jnp.int32, (ROWS, ROWS), 1)
    return jnp.sum(jnp.where((col == row) & (j < i), 1.0, 0.0), axis=0, keepdims=True)


def pack_kernel(emb_far, ids_far, ord_far, own_far, out_ref, slot_ref, emb_ref, ids_ref, ord_ref, own_ref):
    pltpu.sync_copy(emb_far, emb_ref)
    pltpu.sync_copy(ids_far, ids_ref)
    pltpu.sync_copy(ord_far, ord_ref)
    pltpu.sync_copy(own_far, own_ref)
    target = targets(ids_ref[...], own_ref[...])
    rank = rank_among_equal(target)
    pos = (rank * DEVS + target).astype(jnp.int32)
    slot_ref[...] = pos
    emb = emb_ref[...]
    squares = jnp.sum(emb * emb, axis=1, keepdims=True) + 1e-06
    units = (emb * lax.rsqrt(squares)).astype(BF)
    scale = jnp.sqrt(squares).astype(BF)
    lane = lax.broadcasted_iota(jnp.int32, (ROWS, 128), 1)
    scale_lanes = jnp.where(lane == 0, scale.astype(F32), 0.0).astype(BF)
    order = ord_ref[...]
    high = order // 256
    low = order - high * 256
    sub = lax.broadcasted_iota(jnp.int32, (128, ROWS), 0)
    order_lanes = jnp.where(sub == 1, high + 1, jnp.where(sub == 2, low, 0)).astype(F32).astype(BF)
    for k in range(2):
        place = (lax.broadcasted_iota(jnp.int32, (DEVS, ROWS), 0) + k * DEVS == pos).astype(F32).astype(BF)
        rows = pl.ds(k * DEVS, DEVS)
        out_ref[rows, :D] = jnp.dot(place, units, preferred_element_type=F32).astype(BF)
        meta = jnp.dot(place, scale_lanes, preferred_element_type=F32)
        meta = meta + lax.dot_general(place, order_lanes, NT, preferred_element_type=F32)
        out_ref[rows, D:] = meta.astype(BF)


def owner_kernel(rows_ref, center_ref, back_ref):
    total = 2 * DEVS
    meta = rows_ref[:, D:].astype(F32)
    meta_t = jnp.transpose(meta)
    order_col = (meta[:, 1:2] - 1.0) * 256.0 + meta[:, 2:3]
    key_col = jnp.where(order_col >= 0.0, order_col, 1e6)
    order_row = (meta_t[1:2] - 1.0) * 256.0 + meta_t[2:3]
    members = jnp.sum(jnp.where(order_row >= 0.0, 1.0, 0.0))
    keys = rows_ref[:, :D]
    scale = jnp.broadcast_to(meta_t[0:1], (8, total)).astype(BF)
    center = jnp.dot(scale, keys, preferred_element_type=F32)[0:1] / members
    center_ref[...] = center
    length = lax.rsqrt(jnp.sum(center * center, axis=1, keepdims=True) + 1e-06)
    direction = jnp.broadcast_to(center * length, (8, D)).astype(BF)
    aligned = lax.dot_general(direction, keys, NT, preferred_element_type=F32)[0:1]
    back_ref[2:3] = aligned[:, :DEVS]
    back_ref[3:4] = aligned[:, DEVS:]
    block = 256
    for b in range(total // block):
        scores = lax.dot_general(
            keys, rows_ref[pl.ds(b * block, block), :D], NT, preferred_element_type=F32
        )
        earlier = key_col < order_row[:, b * block : (b + 1) * block]
        best = jnp.max(jnp.where(earlier, scores, -1.0), axis=0, keepdims=True)
        k, first = divmod(b * block, DEVS)
        back_ref[k : k + 1, first : first + block] = best


def row_of(col):
    return jnp.transpose(jnp.broadcast_to(col, (col.shape[0], 128)))[:1]


def iota(shape, dim):
    return lax.broadcasted_iota(jnp.int32, shape, dim)


def hot(condition):
    return condition.astype(F32).astype(BF)


def dot(a, b):
    return jnp.dot(a, b, preferred_element_type=F32)


def dot_nt(a, b):
    return lax.dot_general(a, b, NT, preferred_element_type=F32)


def slab_pack_kernel(emb_ref, ids_ref, ord_ref, own_ref, out_ref, slot_ref):
    target = targets(ids_ref[...], own_ref[...])
    rank = rank_among_equal(target).astype(jnp.int32)
    whole = target.astype(jnp.int32)
    slot_ref[...] = rank * DEVS + whole
    z = whole // NQ
    q = whole - z * NQ
    place = rank_among_equal(z.astype(F32)).astype(jnp.int32)
    overflow = jnp.max((place >= FIT).astype(F32), axis=1, keepdims=True)
    left = z * CHUNK_Z + jnp.where(place < NQ, place, place + NQ)
    right = left + jnp.where(place < NQ, NQ, 4)
    left = jnp.where(place < FIT, left, -1)
    right = jnp.where(place < FIT, right, -1)
    emb = emb_ref[...]
    squares = jnp.sum(emb * emb, axis=1, keepdims=True) + 1e-06
    units = (emb * lax.rsqrt(squares)).astype(BF)
    scale = row_of(jnp.sqrt(squares).astype(BF).astype(F32))
    order = ord_ref[...]
    high = order // 256
    low = order - high * 256
    sub = iota((NZ * 4, ROWS), 0)
    value = sub // NZ
    picked = jnp.where(
        value == 0,
        scale,
        jnp.where(value == 1, high, jnp.where(value == 2, low, q * 2 + rank + 1)).astype(F32),
    )
    mine = jnp.where(sub - value * NZ == z, picked, 0.0).astype(BF)
    even = hot(iota((128, ROWS), 0) == place)
    odd = hot(iota((128, ROWS), 0) == place + 64)
    found = [
        (dot_nt(mine[v * NZ : (v + 1) * NZ], even) + dot_nt(mine[(v + 1) * NZ : (v + 2) * NZ], odd)).astype(BF)
        for v in (0, 2)
    ]
    meta = jnp.concatenate(found + [jnp.broadcast_to(overflow, (NZ, 128)).astype(BF)], axis=1)
    rows = iota((SENT, ROWS), 0)
    last = hot(iota((SENT, NZ), 0) == iota((SENT, NZ), 1) * CHUNK_Z + 67)
    sent = dot(hot(rows == left), units[:, :HALF]) + dot(hot(rows == right), units[:, HALF:])
    out_ref[...] = (sent + dot(last, meta)).astype(BF)


def repack_kernel(rows_ref, out_ref):
    main_left = rows_ref[:, :NQ, :].reshape(MAIN, HALF)
    main_right = rows_ref[:, NQ : 2 * NQ, :].reshape(MAIN, HALF)
    tail = rows_ref[:, 2 * NQ :, :].reshape(NZ * 8, HALF)
    meta = dot(hot(iota((NZ, NZ * 8), 1) == iota((NZ, NZ * 8), 0) * 8 + 3), tail)
    flag = jnp.max(meta[:, 256:384])
    pairs = jnp.concatenate([meta[:, :128], meta[:, 128:256]], axis=0).astype(BF)

    def source(shape):
        k = iota(shape, 1)
        t = k - MAIN
        z = jnp.where(t < 0, k // NQ, t // 8)
        place = jnp.where(t < 0, k - z * NQ, NQ + t - (t // 4) * 4)
        return z, place, t

    sub = iota((128, KEPT), 0)
    _, place, _ = source((128, KEPT))
    z, _, _ = source((NZ * 2, KEPT))
    here = iota((NZ * 2, KEPT), 0)
    here = here - (here // NZ) * NZ == z
    evens = jnp.where(here, dot(pairs, hot(sub == place)), 0.0).reshape(2, NZ, KEPT)
    odds = jnp.where(here, dot(pairs, hot(sub == place + 64)), 0.0).reshape(2, NZ, KEPT)
    scale = jnp.sum(evens[0], axis=0, keepdims=True)
    low = jnp.sum(evens[1], axis=0, keepdims=True)
    high = jnp.sum(odds[0], axis=0, keepdims=True)
    code = jnp.sum(odds[1], axis=0, keepdims=True).astype(jnp.int32) - 1
    z, place, t = source((1, KEPT))
    filled = (code >= 0) & (place < FIT)
    q = code // 2
    slot = (code - q * 2) * NZ + z
    is_left = filled & ((t < 0) | (t - (t // 8) * 8 < 4))
    is_right = filled & ((t < 0) | (t - (t // 8) * 8 >= 4))
    left = jnp.where(is_left, q * NQ + slot, -1)
    right = jnp.where(is_right, q * NQ + slot, -1)
    spread = hot(iota((2 * DEVS, MAIN), 0) == left[:, :MAIN])
    rows = iota((2 * DEVS, NZ * 8), 0)
    halves = (
        (dot(spread, main_left) + dot(hot(rows == left[:, MAIN:]), tail)).astype(BF),
        (dot(spread, main_right) + dot(hot(rows == right[:, MAIN:]), tail)).astype(BF),
    )
    for c in range(COLS):
        half, part = divmod(c, COLS // 2)
        block = halves[half][:, part * 128 : (part + 1) * 128]
        out_ref[:, c * NQ : (c + 1) * NQ, :] = block.reshape(NQ, NQ, 128)
    v = iota((8, KEPT), 0)
    eight = jnp.where(v == 0, scale, jnp.where(v == 1, high, jnp.where(v == 2, low, jnp.where(v == 3, 1.0, 0.0))))
    eight = jnp.broadcast_to(eight[None], (NQ, 8, KEPT)).reshape(NQ * 8, KEPT)
    owner = jnp.where(is_left, q, -1)
    mine = jnp.where(iota((NQ * 8, KEPT), 0) // 8 == owner, eight, 0.0).astype(BF)
    details = dot_nt(mine, hot(iota((128, KEPT), 0) == slot))
    sub = iota((NQ * 8, 128), 0)
    details = details + jnp.where(sub - (sub // 8) * 8 == 4, flag, 0.0)
    out_ref[:, COLS * NQ :, :] = details.astype(BF).reshape(NQ, 8, 128)


def slab_owner_kernel(rows_ref, center_ref, back_ref, flag_ref, keys_ref):
    total = 2 * DEVS
    for c in range(COLS):
        keys_ref[:, c * 128 : (c + 1) * 128] = rows_ref[:, c * NQ : (c + 1) * NQ, :].reshape(total, 128)
    details = rows_ref[:, COLS * NQ :, :].reshape(NQ * 8, 128)
    n = iota((128, total), 1)
    along = dot(details, hot(iota((128, total), 0) == n - (n // NQ) * NQ))
    here = iota((NQ * 8, total), 0) // 8 == iota((NQ * 8, total), 1) // NQ
    values = jnp.sum(jnp.where(here, along, 0.0).reshape(NQ, 8, total), axis=0)
    flag_ref[...] = jnp.broadcast_to(jnp.max(values[4:5], axis=1, keepdims=True), (1, 128))
    order_row = values[1:2] * 256.0 + values[2:3]
    members = jnp.sum(values[3:4], axis=1, keepdims=True)
    key_col = column(jnp.where(values[3:4] > 0.0, order_row, 1e6))
    scale = jnp.broadcast_to(values[0:1], (8, total)).astype(BF)
    center = dot(scale, keys_ref[...])[0:1] / members
    center_ref[...] = center
    length = lax.rsqrt(jnp.sum(center * center, axis=1, keepdims=True) + 1e-06)
    direction = jnp.broadcast_to(center * length, (8, D)).astype(BF)
    back_ref[1:2] = dot_nt(direction, keys_ref[...])[0:1]
    key_row = jnp.where(values[3:4] > 0.0, order_row, 1e6)
    block = 256
    best = []
    across = []
    for b in range(total // block):
        mine = slice(b * block, (b + 1) * block)
        row = None
        for a in range(b + 1):
            other = slice(a * block, (a + 1) * block)
            scores = dot_nt(keys_ref[other, :], keys_ref[mine, :])
            found = jnp.where(key_col[other] < order_row[:, mine], scores, -1.0)
            found = jnp.max(found, axis=0, keepdims=True)
            row = found if row is None else jnp.maximum(row, found)
            if a < b:
                found = jnp.where(key_row[:, mine] < key_col[other], scores, -1.0)
                found = jnp.max(found, axis=1, keepdims=True)
                across[a] = found if across[a] is None else jnp.maximum(across[a], found)
        best.append(row)
        across.append(None)
    lane = iota((block, 128), 1)
    mirrored = jnp.full((block, 128), -1.0)
    for a, found in enumerate(across[:-1]):
        mirrored = jnp.where(lane == a, found, mirrored)
    mirrored = jnp.transpose(mirrored)
    for b, row in enumerate(best):
        back_ref[0:1, b * block : (b + 1) * block] = jnp.maximum(row, mirrored[b : b + 1])


def unpack_kernel(got_ref, slot_ref, near_ref, align_ref):
    slot = slot_ref[...]
    rank = slot // DEVS
    target = slot - rank * DEVS
    z = target // NQ
    q = target - z * NQ
    from_z = (iota((NZ, ROWS), 0) == z).astype(F32)
    column_of = lax.dot_general(
        got_ref[...], from_z, TN, precision=lax.Precision.HIGHEST, preferred_element_type=F32
    )
    sub = iota((128, ROWS), 0)
    near_ref[...] = jnp.sum(jnp.where(sub == rank * NQ + q, column_of, 0.0), axis=0, keepdims=True)
    align_ref[...] = jnp.sum(jnp.where(sub == (rank + 2) * NQ + q, column_of, 0.0), axis=0, keepdims=True)


def full_exchange(embeddings, ids_row, orders_row, owner_row):
    sds = jax.ShapeDtypeStruct
    packed, _ = call(
        pack_kernel,
        [sds((2 * DEVS, W), BF), sds((1, ROWS), jnp.int32)],
        embeddings,
        ids_row,
        orders_row,
        owner_row,
        scratch=[
            pltpu.VMEM((ROWS, D), F32),
            pltpu.VMEM((1, ROWS), jnp.int32),
            pltpu.VMEM((1, ROWS), jnp.int32),
            pltpu.VMEM((1, DEVS), jnp.int32),
        ],
        far=4,
    )
    send = packed.reshape(2, DEVS, W).transpose(1, 0, 2)
    got = lax.all_to_all(send, ALL, split_axis=0, concat_axis=0, tiled=True)
    rows = got.transpose(1, 0, 2).reshape(2 * DEVS, W)
    center, back = call(owner_kernel, [sds((1, D), F32), sds((4, DEVS), F32)], rows)
    return center, back.reshape(2, 2, NZ, NQ).transpose(0, 3, 1, 2).reshape(2, 2 * DEVS)


def local(embeddings, cluster_ids, orders, owner):
    sds = jax.ShapeDtypeStruct
    ids_row = cluster_ids.reshape(1, ROWS)
    orders_row = orders.reshape(1, ROWS)
    owner_row = owner.reshape(1, DEVS)
    packed, slot = call(
        slab_pack_kernel,
        [sds((SENT, HALF), BF), sds((1, ROWS), jnp.int32)],
        embeddings,
        ids_row,
        orders_row,
        owner_row,
    )
    got = lax.all_to_all(packed.reshape(NZ, CHUNK_Z, HALF), "z", split_axis=0, concat_axis=0, tiled=True)
    (moved,) = call(repack_kernel, [sds((NQ, CHUNK, 128), BF)], got)
    rows = lax.all_to_all(moved, SLAB, split_axis=0, concat_axis=0, tiled=True)
    center, back, flag = call(
        slab_owner_kernel,
        [sds((1, D), F32), sds((2, 2 * DEVS), F32), sds((1, 128), F32)],
        rows,
        scratch=[pltpu.VMEM((2 * DEVS, D), BF)],
    )
    flag, *arguments = lax.optimization_barrier((flag, embeddings, ids_row, orders_row, owner_row))
    center, back = lax.cond(
        flag[0, 0] > 0.0,
        lambda: full_exchange(*arguments),
        lambda: (center, back),
    )
    back = back.reshape(2, NQ, NQ).transpose(1, 0, 2).reshape(NQ, 1, 2 * NQ)
    back = lax.all_to_all(back, SLAB, split_axis=0, concat_axis=0, tiled=True)
    back = back.reshape(NQ, 4, NZ).transpose(2, 1, 0).reshape(NZ, 1, 4 * NQ)
    back = lax.all_to_all(back, "z", split_axis=0, concat_axis=0, tiled=True)
    near, align = call(
        unpack_kernel,
        [sds((1, ROWS), F32), sds((1, ROWS), F32)],
        back.reshape(NZ, 4 * NQ),
        slot,
    )
    return (center, near.reshape(ROWS), align.reshape(ROWS))


def solution(mesh):
    fine = Mesh(mesh.devices.reshape(16, 4, 2, 4), ALL)
    return jax.shard_map(
        local,
        mesh=fine,
        in_specs=(P(ALL, None), P(ALL), P(ALL), P()),
        out_specs=(P(ALL, None), P(ALL), P(ALL)),
        check_vma=False,
    )
```

```python
import jax
import jax.numpy as jnp
from jax import lax
from jax.experimental import pallas as pl
from jax.experimental.pallas import tpu as pltpu
from jax.sharding import Mesh
from jax.sharding import PartitionSpec as P

ALL = ("z", "y", "core", "x")
SLAB = ("y", "core", "x")
NZ = 16
NQ = 32
DEVS = NZ * NQ
ROWS = 256
D = 768
W = D + 128
BF = jnp.bfloat16
F32 = jnp.float32
NT = (((1,), (1,)), ((), ()))
TN = (((0,), (0,)), ((), ()))
FIT = 35
HALF = D // 2
CHUNK_Z = 2 * (FIT + 1)
SENT = NZ * CHUNK_Z
MAIN = NZ * NQ
KEPT = MAIN + NZ * 8
COLS = D // 128
CHUNK = COLS * NQ + 8


def column(row):
    return jnp.transpose(jnp.broadcast_to(row, (128, row.shape[1])))[:, :1]


def call(kernel, shapes, *args, scratch=(), far=0):
    return pl.pallas_call(
        kernel,
        out_shape=shapes,
        scratch_shapes=scratch,
        compiler_params=pltpu.CompilerParams(vmem_limit_bytes=24 * 2**20),
        in_specs=[pl.BlockSpec(memory_space=pltpu.HBM if i < far else pltpu.VMEM) for i in range(len(args))],
        out_specs=[pl.BlockSpec(memory_space=pltpu.VMEM) for _ in shapes],
    )(*args)


def targets(ids_row, owner_row):
    hot = (lax.broadcasted_iota(jnp.int32, (DEVS, ROWS), 0) == ids_row).astype(F32).astype(BF)
    high = owner_row // 16
    low = owner_row - high * 16
    sub = lax.broadcasted_iota(jnp.int32, (8, DEVS), 0)
    digits = jnp.where(sub == 0, high, jnp.where(sub == 1, low, 0)).astype(F32).astype(BF)
    found = jnp.dot(digits, hot, preferred_element_type=F32)
    return found[0:1] * 16.0 + found[1:2]


def rank_among_equal(row):
    col = column(row)
    j = lax.broadcasted_iota(jnp.int32, (ROWS, ROWS), 0)
    i = lax.broadcasted_iota(jnp.int32, (ROWS, ROWS), 1)
    return jnp.sum(jnp.where((col == row) & (j < i), 1.0, 0.0), axis=0, keepdims=True)


def pack_kernel(emb_far, ids_far, ord_far, own_far, out_ref, slot_ref, emb_ref, ids_ref, ord_ref, own_ref):
    pltpu.sync_copy(emb_far, emb_ref)
    pltpu.sync_copy(ids_far, ids_ref)
    pltpu.sync_copy(ord_far, ord_ref)
    pltpu.sync_copy(own_far, own_ref)
    target = targets(ids_ref[...], own_ref[...])
    rank = rank_among_equal(target)
    pos = (rank * DEVS + target).astype(jnp.int32)
    slot_ref[...] = pos
    emb = emb_ref[...]
    squares = jnp.sum(emb * emb, axis=1, keepdims=True) + 1e-06
    units = (emb * lax.rsqrt(squares)).astype(BF)
    scale = jnp.sqrt(squares).astype(BF)
    lane = lax.broadcasted_iota(jnp.int32, (ROWS, 128), 1)
    scale_lanes = jnp.where(lane == 0, scale.astype(F32), 0.0).astype(BF)
    order = ord_ref[...]
    high = order // 256
    low = order - high * 256
    sub = lax.broadcasted_iota(jnp.int32, (128, ROWS), 0)
    order_lanes = jnp.where(sub == 1, high + 1, jnp.where(sub == 2, low, 0)).astype(F32).astype(BF)
    for k in range(2):
        place = (lax.broadcasted_iota(jnp.int32, (DEVS, ROWS), 0) + k * DEVS == pos).astype(F32).astype(BF)
        rows = pl.ds(k * DEVS, DEVS)
        out_ref[rows, :D] = jnp.dot(place, units, preferred_element_type=F32).astype(BF)
        meta = jnp.dot(place, scale_lanes, preferred_element_type=F32)
        meta = meta + lax.dot_general(place, order_lanes, NT, preferred_element_type=F32)
        out_ref[rows, D:] = meta.astype(BF)


def owner_kernel(rows_ref, center_ref, back_ref):
    total = 2 * DEVS
    meta = rows_ref[:, D:].astype(F32)
    meta_t = jnp.transpose(meta)
    order_col = (meta[:, 1:2] - 1.0) * 256.0 + meta[:, 2:3]
    key_col = jnp.where(order_col >= 0.0, order_col, 1e6)
    order_row = (meta_t[1:2] - 1.0) * 256.0 + meta_t[2:3]
    members = jnp.sum(jnp.where(order_row >= 0.0, 1.0, 0.0))
    keys = rows_ref[:, :D]
    scale = jnp.broadcast_to(meta_t[0:1], (8, total)).astype(BF)
    center = jnp.dot(scale, keys, preferred_element_type=F32)[0:1] / members
    center_ref[...] = center
    length = lax.rsqrt(jnp.sum(center * center, axis=1, keepdims=True) + 1e-06)
    direction = jnp.broadcast_to(center * length, (8, D)).astype(BF)
    aligned = lax.dot_general(direction, keys, NT, preferred_element_type=F32)[0:1]
    back_ref[2:3] = aligned[:, :DEVS]
    back_ref[3:4] = aligned[:, DEVS:]
    block = 256
    for b in range(total // block):
        scores = lax.dot_general(
            keys, rows_ref[pl.ds(b * block, block), :D], NT, preferred_element_type=F32
        )
        earlier = key_col < order_row[:, b * block : (b + 1) * block]
        best = jnp.max(jnp.where(earlier, scores, -1.0), axis=0, keepdims=True)
        k, first = divmod(b * block, DEVS)
        back_ref[k : k + 1, first : first + block] = best


def row_of(col):
    return jnp.transpose(jnp.broadcast_to(col, (col.shape[0], 128)))[:1]


def iota(shape, dim):
    return lax.broadcasted_iota(jnp.int32, shape, dim)


def hot(condition):
    return condition.astype(F32).astype(BF)


def dot(a, b):
    return jnp.dot(a, b, preferred_element_type=F32)


def dot_nt(a, b):
    return lax.dot_general(a, b, NT, preferred_element_type=F32)


def slab_pack_kernel(emb_ref, ids_ref, ord_ref, own_ref, out_ref, slot_ref):
    target = targets(ids_ref[...], own_ref[...])
    rank = rank_among_equal(target).astype(jnp.int32)
    whole = target.astype(jnp.int32)
    slot_ref[...] = rank * DEVS + whole
    z = whole // NQ
    q = whole - z * NQ
    place = rank_among_equal(z.astype(F32)).astype(jnp.int32)
    overflow = jnp.max((place >= FIT).astype(F32), axis=1, keepdims=True)
    left = z * CHUNK_Z + jnp.where(place < NQ, place, place + NQ)
    right = left + jnp.where(place < NQ, NQ, 4)
    left = jnp.where(place < FIT, left, -1)
    right = jnp.where(place < FIT, right, -1)
    emb = emb_ref[...]
    squares = jnp.sum(emb * emb, axis=1, keepdims=True) + 1e-06
    units = (emb * lax.rsqrt(squares)).astype(BF)
    scale = row_of(jnp.sqrt(squares).astype(BF).astype(F32))
    order = ord_ref[...]
    high = order // 256
    low = order - high * 256
    sub = iota((NZ * 4, ROWS), 0)
    value = sub // NZ
    picked = jnp.where(
        value == 0,
        scale,
        jnp.where(value == 1, high, jnp.where(value == 2, low, q * 2 + rank + 1)).astype(F32),
    )
    mine = jnp.where(sub - value * NZ == z, picked, 0.0).astype(BF)
    even = hot(iota((128, ROWS), 0) == place)
    odd = hot(iota((128, ROWS), 0) == place + 64)
    found = [
        (dot_nt(mine[v * NZ : (v + 1) * NZ], even) + dot_nt(mine[(v + 1) * NZ : (v + 2) * NZ], odd)).astype(BF)
        for v in (0, 2)
    ]
    meta = jnp.concatenate(found + [jnp.broadcast_to(overflow, (NZ, 128)).astype(BF)], axis=1)
    rows = iota((SENT, ROWS), 0)
    last = hot(iota((SENT, NZ), 0) == iota((SENT, NZ), 1) * CHUNK_Z + 67)
    sent = dot(hot(rows == left), units[:, :HALF]) + dot(hot(rows == right), units[:, HALF:])
    out_ref[...] = (sent + dot(last, meta)).astype(BF)


def repack_kernel(rows_ref, out_ref):
    main_left = rows_ref[:, :NQ, :].reshape(MAIN, HALF)
    main_right = rows_ref[:, NQ : 2 * NQ, :].reshape(MAIN, HALF)
    tail = rows_ref[:, 2 * NQ :, :].reshape(NZ * 8, HALF)
    meta = dot(hot(iota((NZ, NZ * 8), 1) == iota((NZ, NZ * 8), 0) * 8 + 3), tail)
    flag = jnp.max(meta[:, 256:384])
    pairs = jnp.concatenate([meta[:, :128], meta[:, 128:256]], axis=0).astype(BF)

    def source(shape):
        k = iota(shape, 1)
        t = k - MAIN
        z = jnp.where(t < 0, k // NQ, t // 8)
        place = jnp.where(t < 0, k - z * NQ, NQ + t - (t // 4) * 4)
        return z, place, t

    sub = iota((128, KEPT), 0)
    _, place, _ = source((128, KEPT))
    z, _, _ = source((NZ * 2, KEPT))
    here = iota((NZ * 2, KEPT), 0)
    here = here - (here // NZ) * NZ == z
    evens = jnp.where(here, dot(pairs, hot(sub == place)), 0.0).reshape(2, NZ, KEPT)
    odds = jnp.where(here, dot(pairs, hot(sub == place + 64)), 0.0).reshape(2, NZ, KEPT)
    scale = jnp.sum(evens[0], axis=0, keepdims=True)
    low = jnp.sum(evens[1], axis=0, keepdims=True)
    high = jnp.sum(odds[0], axis=0, keepdims=True)
    code = jnp.sum(odds[1], axis=0, keepdims=True).astype(jnp.int32) - 1
    z, place, t = source((1, KEPT))
    filled = (code >= 0) & (place < FIT)
    q = code // 2
    slot = (code - q * 2) * NZ + z
    is_left = filled & ((t < 0) | (t - (t // 8) * 8 < 4))
    is_right = filled & ((t < 0) | (t - (t // 8) * 8 >= 4))
    left = jnp.where(is_left, q * NQ + slot, -1)
    right = jnp.where(is_right, q * NQ + slot, -1)
    spread = hot(iota((2 * DEVS, MAIN), 0) == left[:, :MAIN])
    rows = iota((2 * DEVS, NZ * 8), 0)
    halves = (
        (dot(spread, main_left) + dot(hot(rows == left[:, MAIN:]), tail)).astype(BF),
        (dot(spread, main_right) + dot(hot(rows == right[:, MAIN:]), tail)).astype(BF),
    )
    for c in range(COLS):
        half, part = divmod(c, COLS // 2)
        block = halves[half][:, part * 128 : (part + 1) * 128]
        out_ref[:, c * NQ : (c + 1) * NQ, :] = block.reshape(NQ, NQ, 128)
    v = iota((8, KEPT), 0)
    eight = jnp.where(v == 0, scale, jnp.where(v == 1, high, jnp.where(v == 2, low, jnp.where(v == 3, 1.0, 0.0))))
    eight = jnp.broadcast_to(eight[None], (NQ, 8, KEPT)).reshape(NQ * 8, KEPT)
    owner = jnp.where(is_left, q, -1)
    mine = jnp.where(iota((NQ * 8, KEPT), 0) // 8 == owner, eight, 0.0).astype(BF)
    details = dot_nt(mine, hot(iota((128, KEPT), 0) == slot))
    sub = iota((NQ * 8, 128), 0)
    details = details + jnp.where(sub - (sub // 8) * 8 == 4, flag, 0.0)
    out_ref[:, COLS * NQ :, :] = details.astype(BF).reshape(NQ, 8, 128)


def slab_owner_kernel(rows_ref, center_ref, back_ref, flag_ref, keys_ref):
    total = 2 * DEVS
    for c in range(COLS):
        keys_ref[:, c * 128 : (c + 1) * 128] = rows_ref[:, c * NQ : (c + 1) * NQ, :].reshape(total, 128)
    details = rows_ref[:, COLS * NQ :, :].reshape(NQ * 8, 128)
    n = iota((128, total), 1)
    along = dot(details, hot(iota((128, total), 0) == n - (n // NQ) * NQ))
    here = iota((NQ * 8, total), 0) // 8 == iota((NQ * 8, total), 1) // NQ
    values = jnp.sum(jnp.where(here, along, 0.0).reshape(NQ, 8, total), axis=0)
    flag_ref[...] = jnp.broadcast_to(jnp.max(values[4:5], axis=1, keepdims=True), (1, 128))
    order_row = values[1:2] * 256.0 + values[2:3]
    members = jnp.sum(values[3:4], axis=1, keepdims=True)
    key_col = column(jnp.where(values[3:4] > 0.0, order_row, 1e6))
    key_row = jnp.where(values[3:4] > 0.0, order_row, 1e6)
    block = 256
    best = []
    across = []
    for b in range(total // block):
        mine = slice(b * block, (b + 1) * block)
        row = None
        for a in range(b + 1):
            other = slice(a * block, (a + 1) * block)
            scores = dot_nt(keys_ref[other, :], keys_ref[mine, :])
            found = jnp.where(key_col[other] < order_row[:, mine], scores, -1.0)
            found = jnp.max(found, axis=0, keepdims=True)
            row = found if row is None else jnp.maximum(row, found)
            if a < b:
                found = jnp.where(key_row[:, mine] < key_col[other], scores, -1.0)
                found = jnp.max(found, axis=1, keepdims=True)
                across[a] = found if across[a] is None else jnp.maximum(across[a], found)
        best.append(row)
        across.append(None)
    lane = iota((block, 128), 1)
    mirrored = jnp.full((block, 128), -1.0)
    for a, found in enumerate(across[:-1]):
        mirrored = jnp.where(lane == a, found, mirrored)
    mirrored = jnp.transpose(mirrored)
    for b, row in enumerate(best):
        back_ref[0:1, b * block : (b + 1) * block] = jnp.maximum(row, mirrored[b : b + 1])
    scale = jnp.broadcast_to(values[0:1], (8, total)).astype(BF)
    center = dot(scale, keys_ref[...])[0:1] / members
    center_ref[...] = center
    length = lax.rsqrt(jnp.sum(center * center, axis=1, keepdims=True) + 1e-06)
    direction = jnp.broadcast_to(center * length, (8, D)).astype(BF)
    back_ref[1:2] = dot_nt(direction, keys_ref[...])[0:1]


def unpack_kernel(got_ref, slot_ref, near_ref, align_ref):
    slot = slot_ref[...]
    rank = slot // DEVS
    target = slot - rank * DEVS
    z = target // NQ
    q = target - z * NQ
    from_z = (iota((NZ, ROWS), 0) == z).astype(F32)
    column_of = lax.dot_general(
        got_ref[...], from_z, TN, precision=lax.Precision.HIGHEST, preferred_element_type=F32
    )
    sub = iota((128, ROWS), 0)
    near_ref[...] = jnp.sum(jnp.where(sub == rank * NQ + q, column_of, 0.0), axis=0, keepdims=True)
    align_ref[...] = jnp.sum(jnp.where(sub == (rank + 2) * NQ + q, column_of, 0.0), axis=0, keepdims=True)


def full_exchange(embeddings, ids_row, orders_row, owner_row):
    sds = jax.ShapeDtypeStruct
    packed, _ = call(
        pack_kernel,
        [sds((2 * DEVS, W), BF), sds((1, ROWS), jnp.int32)],
        embeddings,
        ids_row,
        orders_row,
        owner_row,
        scratch=[
            pltpu.VMEM((ROWS, D), F32),
            pltpu.VMEM((1, ROWS), jnp.int32),
            pltpu.VMEM((1, ROWS), jnp.int32),
            pltpu.VMEM((1, DEVS), jnp.int32),
        ],
        far=4,
    )
    send = packed.reshape(2, DEVS, W).transpose(1, 0, 2)
    got = lax.all_to_all(send, ALL, split_axis=0, concat_axis=0, tiled=True)
    rows = got.transpose(1, 0, 2).reshape(2 * DEVS, W)
    center, back = call(owner_kernel, [sds((1, D), F32), sds((4, DEVS), F32)], rows)
    return center, back.reshape(2, 2, NZ, NQ).transpose(0, 3, 1, 2).reshape(2, 2 * DEVS)


def local(embeddings, cluster_ids, orders, owner):
    sds = jax.ShapeDtypeStruct
    ids_row = cluster_ids.reshape(1, ROWS)
    orders_row = orders.reshape(1, ROWS)
    owner_row = owner.reshape(1, DEVS)
    packed, slot = call(
        slab_pack_kernel,
        [sds((SENT, HALF), BF), sds((1, ROWS), jnp.int32)],
        embeddings,
        ids_row,
        orders_row,
        owner_row,
    )
    got = lax.all_to_all(packed.reshape(NZ, CHUNK_Z, HALF), "z", split_axis=0, concat_axis=0, tiled=True)
    (moved,) = call(repack_kernel, [sds((NQ, CHUNK, 128), BF)], got)
    rows = lax.all_to_all(moved, SLAB, split_axis=0, concat_axis=0, tiled=True)
    center, back, flag = call(
        slab_owner_kernel,
        [sds((1, D), F32), sds((2, 2 * DEVS), F32), sds((1, 128), F32)],
        rows,
        scratch=[pltpu.VMEM((2 * DEVS, D), BF)],
    )
    flag, *arguments = lax.optimization_barrier((flag, embeddings, ids_row, orders_row, owner_row))
    center, back = lax.cond(
        flag[0, 0] > 0.0,
        lambda: full_exchange(*arguments),
        lambda: (center, back),
    )
    back = back.reshape(2, NQ, NQ).transpose(1, 0, 2).reshape(NQ, 1, 2 * NQ)
    back = lax.all_to_all(back, SLAB, split_axis=0, concat_axis=0, tiled=True)
    back = back.reshape(NQ, 4, NZ).transpose(2, 1, 0).reshape(NZ, 1, 4 * NQ)
    back = lax.all_to_all(back, "z", split_axis=0, concat_axis=0, tiled=True)
    near, align = call(
        unpack_kernel,
        [sds((1, ROWS), F32), sds((1, ROWS), F32)],
        back.reshape(NZ, 4 * NQ),
        slot,
    )
    return (center, near.reshape(ROWS), align.reshape(ROWS))


def solution(mesh):
    fine = Mesh(mesh.devices.reshape(16, 4, 2, 4), ALL)
    return jax.shard_map(
        local,
        mesh=fine,
        in_specs=(P(ALL, None), P(ALL), P(ALL), P()),
        out_specs=(P(ALL, None), P(ALL), P(ALL)),
        check_vma=False,
    )
```
